32 devices in a mesh: sky: 4 (over y, x), visit: 4 (over z), patch: 2 (over core).
Axes of the slice: x: 2, y: 2, z: 4, core: 2. Of those that a mesh axis runs over, the one named last changes fastest.
Arguments:
- template_store: float32 [4, 128, 2048], P('visit', 'patch', 'sky'), may hold values from -6 to 6
- science: float32 [4, 128, 2048], P('visit', 'patch', 'sky'), may hold values from -40 to 40
- owner_visit: int32 [4, 2], P('sky', 'patch'), may hold values from 0 to 3, as said below
- stamp_offset: int32 [2, 4, 2, 32], P(None, 'visit', 'patch', 'sky'), may hold values from 0 to 32
Outputs:
- difference: float32 [4, 128, 2048], P('visit', 'patch', 'sky')
The draws below stay inside these ranges and needn't reach their ends.
Inputs may be any that keep to these rules, and one draw needn't show every extreme that they name: owner_visit[s, p] = (owner_visit[s, 0] + p) mod 4; only that visit's slot of template_store holds the current coadd of sky tile s, patch p.
All inputs are finite; a program needn't handle non-finite values.
Results may differ from the reference program's by a relative error of at most 0.0003.
Values sent between devices are 32-bit elements; how exact they have to be, the bound alone decides.
A program may use at most 128 MiB of HBM per device.

```python
import math
import jax
import jax.numpy as jnp
from jax import lax

PR = 64
PC = 512
HALF = 15
NBASIS = 25
CELL = 64
STAMP = 32
TILES = 4
VISITS = 4
PATCHES = 2
NR = 128
NC = 2048
RC = 1
CC = 8


blur_spread = 2.0


blur_reach = 6


def owner_table(key):
    base_visit = jax.random.randint(jax.random.fold_in(key, 11), (TILES, 1), 0, VISITS)
    return (base_visit + jnp.arange(PATCHES)[None, :]) % VISITS


def gauss_profile(spread_px, tap_reach):
    offsets = jnp.arange(2 * tap_reach + 1).astype(jnp.float32) - tap_reach
    ratio = offsets / spread_px
    profile = jnp.exp(-0.5 * ratio * ratio)
    return profile / jnp.sum(profile, axis=-1, keepdims=True)


def blur_rows(values, profile, tap_reach):
    length = values.shape[1] - 2 * tap_reach
    summed = profile[:, 0, None, None] * values[:, 0:length, :]
    for tap_at in range(1, 2 * tap_reach + 1):
        summed = summed + profile[:, tap_at, None, None] * values[:, tap_at:tap_at + length, :]
    return summed


def blur_cols(values, profile, tap_reach):
    length = values.shape[2] - 2 * tap_reach
    summed = profile[:, 0, None, None] * values[:, :, 0:length]
    for tap_at in range(1, 2 * tap_reach + 1):
        summed = summed + profile[:, tap_at, None, None] * values[:, :, tap_at:tap_at + length]
    return summed


def coadd_slots(key):
    draw_key = jax.random.fold_in(key, 23)
    grid_shape = (VISITS, NR + 2 * blur_reach, NC + 2 * blur_reach)
    speckle = jax.random.normal(draw_key, grid_shape, jnp.float32)
    profile = gauss_profile(blur_spread, blur_reach)[None]
    blurred = blur_cols(blur_rows(speckle, profile, blur_reach), profile, blur_reach)
    blurred = blurred / jnp.sum(profile * profile)
    return jnp.clip(blurred, -6.0, 6.0)


def draw_template_store(key, part):
    return coadd_slots(key)


def draw_owner_visit(key, part):
    return owner_table(key).astype(jnp.int32)


def draw_science(key, part):
    slot_values = coadd_slots(key)
    owners = owner_table(key).astype(jnp.int32)
    pixel_owner = jnp.repeat(jnp.repeat(owners.T, PR, axis=0), PC, axis=1)
    current = jnp.take_along_axis(slot_values, pixel_owner[None], axis=0)[0]
    padded = jnp.pad(current, HALF)[None]
    visit_spread = (4.0 + 0.3 * jnp.arange(VISITS).astype(jnp.float32))[:, None]
    profile = gauss_profile(visit_spread, HALF)
    matched_sky = blur_cols(blur_rows(padded, profile, HALF), profile, HALF)
    column_ramp = 1.0 + 2.0 * jnp.arange(NC).astype(jnp.float32) / max(NC - 1, 1)
    visit_gain = 1.5 + 0.75 * jnp.arange(VISITS).astype(jnp.float32)
    noise_field = 0.5 * jax.random.normal(jax.random.fold_in(key, 37), (VISITS, NR, NC), jnp.float32)
    values = visit_gain[:, None, None] * column_ramp[None, None, :] * matched_sky + noise_field
    return jnp.clip(values, -40.0, 40.0)


def set_ends(values, key, smallest, top_value):
    longest = values.shape.index(max(values.shape))
    spots = []
    for shift in (0, 1):
        where = [jax.random.randint(jax.random.fold_in(key, axis), (), 0, length) for axis, length in enumerate(values.shape)]
        where[longest] = (where[longest] + shift) % values.shape[longest]
        spots.append(tuple(where))
    return values.at[spots[0]].set(smallest).at[spots[1]].set(top_value)


def setup_inputs(seed: int = 0) -> dict:
    arg_keys = jax.random.split(jax.random.key(seed), 5)
    template_store = draw_template_store(jax.random.fold_in(arg_keys[4], 71), 0)
    science = draw_science(jax.random.fold_in(arg_keys[4], 71), 0)
    owner_visit = draw_owner_visit(jax.random.fold_in(arg_keys[4], 71), 0)
    stamp_offset = set_ends(jax.random.randint(arg_keys[3], (2, VISITS, RC * PATCHES, CC * TILES), 0, CELL - STAMP + 1), jax.random.fold_in(arg_keys[3], 1), 0, CELL - STAMP).astype(jnp.int32)
    return {"template_store": template_store, "science": science, "owner_visit": owner_visit, "stamp_offset": stamp_offset}


kernel_sigma = 5.0
highest = lax.Precision.HIGHEST

def filter_bank():
    tap_offset = jnp.arange(2 * HALF + 1).astype(jnp.float32) - HALF
    scaled = tap_offset / kernel_sigma
    envelope = jnp.exp(-0.5 * scaled * scaled)
    square = scaled * scaled
    polynoms = [jnp.ones_like(scaled), 2.0 * scaled, 4.0 * square - 2.0, 8.0 * square * scaled - 12.0 * scaled, 16.0 * square * square - 48.0 * square + 12.0]
    shaped = jnp.stack(polynoms) * envelope[None, :]
    filters = shaped / jnp.sqrt(lax.optimization_barrier(jnp.sum(shaped * shaped, axis=1, keepdims=True)))
    return (filters, lax.optimization_barrier(jnp.sum(filters, axis=1)))

def solve_small(matrix, targets):
    count = matrix.shape[0]
    order = jnp.arange(count)
    remain = matrix
    factor_cols = []
    for column_at in range(count):
        pivot = jnp.sqrt(remain[column_at, column_at])
        column = jnp.where((order >= column_at)[:, None], remain[:, column_at] / pivot[None, :], 0.0)
        factor_cols.append(column)
        remain = remain - column[:, None, :] * column[None, :, :]
    factor = jnp.stack(factor_cols, axis=1)
    answer = targets
    for column_at in range(count):
        solved = answer[column_at] / factor[column_at, column_at][None, :]
        update = factor[:, column_at][:, None, :] * solved[None]
        answer = jnp.where((order > column_at)[:, None, None], answer - update, answer)
        answer = jnp.where((order == column_at)[:, None, None], solved[None], answer)
    for column_at in reversed(range(count)):
        solved = answer[column_at] / factor[column_at, column_at][None, :]
        update = factor[column_at, :][:, None, :] * solved[None]
        answer = jnp.where((order < column_at)[:, None, None], answer - update, answer)
        answer = jnp.where((order == column_at)[:, None, None], solved[None], answer)
    return answer

def reference(template_store, science, owner_visit, stamp_offset):
    filters, tap_sums = filter_bank()
    flux_vector = (tap_sums[:, None] * tap_sums[None, :]).reshape(-1)
    pixel_owner = jnp.repeat(jnp.repeat(owner_visit.T, PR, axis=0), PC, axis=1)
    coadd_image = jnp.zeros((NR, NC), dtype=template_store.dtype)
    for visit_at in range(VISITS):
        coadd_image = coadd_image + jnp.where(pixel_owner == visit_at, template_store[visit_at], 0.0)
    padded = jnp.pad(coadd_image, HALF)
    local = jnp.arange(CELL).astype(jnp.int32)

    def one_patch(patch_id):
        visit_at = patch_id // (PATCHES * TILES)
        patch_at = patch_id // TILES % PATCHES
        tile_at = patch_id % TILES
        row_first = (patch_at * PR).astype(jnp.int32)
        col_first = (tile_at * PC).astype(jnp.int32)
        zero_at = jnp.zeros((), jnp.int32)
        extended = lax.dynamic_slice(padded, (row_first, col_first), (PR + 2 * HALF, PC + 2 * HALF))
        image = lax.dynamic_slice(science, (visit_at.astype(jnp.int32), row_first, col_first), (1, PR, PC))[0]
        offsets = lax.dynamic_slice(stamp_offset, (zero_at, visit_at.astype(jnp.int32), (patch_at * RC).astype(jnp.int32), (tile_at * CC).astype(jnp.int32)), (2, 1, RC, CC))[:, 0]
        columns_done = filters[:, 0, None, None] * extended[None, :, 0:PC]
        for tap_at in range(1, 2 * HALF + 1):
            columns_done = columns_done + filters[:, tap_at, None, None] * extended[None, :, tap_at:tap_at + PC]
        basis_full = filters[None, :, 0, None, None] * columns_done[:, None, 0:PR, :]
        for tap_at in range(1, 2 * HALF + 1):
            basis_full = basis_full + filters[None, :, tap_at, None, None] * columns_done[:, None, tap_at:tap_at + PR, :]
        basis_cells = basis_full.reshape(NBASIS, RC, CELL, CC, CELL)
        row_off = offsets[0]
        col_off = offsets[1]
        in_y = (local[None, :, None] >= row_off[:, None, :]) & (local[None, :, None] < row_off[:, None, :] + STAMP)
        in_x = (local[None, :, None] >= col_off[:, None, :]) & (local[None, :, None] < col_off[:, None, :] + STAMP)
        in_stamp = (in_y[:, :, :, None] & jnp.transpose(in_x, (0, 2, 1))[:, None, :, :]).astype(image.dtype)
        masked = basis_cells * in_stamp[None]
        gram_matrix = jnp.einsum('krycx,lrycx->klrc', masked, basis_cells, precision=highest).reshape(NBASIS, NBASIS, RC * CC)
        right_side = jnp.einsum('krycx,rycx->krc', masked, image.reshape(RC, CELL, CC, CELL), precision=highest).reshape(NBASIS, RC * CC)
        targets = jnp.stack([right_side, jnp.broadcast_to(flux_vector[:, None], right_side.shape)], axis=1)
        answer = solve_small(gram_matrix, targets)
        weights = answer[:, 0]
        unit_sol = answer[:, 1]
        fitted = jnp.einsum('krycx,krc->rycx', basis_cells, weights.reshape(NBASIS, RC, CC), precision=highest)
        unit_match = jnp.einsum('krycx,krc->rycx', basis_cells, unit_sol.reshape(NBASIS, RC, CC), precision=highest)
        flux_sums = jnp.einsum('k,kc->c', flux_vector, weights, precision=highest)
        curvature = jnp.einsum('k,kc->c', flux_vector, unit_sol, precision=highest)
        return (fitted, unit_match, flux_sums, curvature)
    total_patches = VISITS * PATCHES * TILES
    group_size = math.gcd(8, total_patches)
    patch_ids = jnp.arange(total_patches).astype(jnp.int32).reshape(-1, group_size)
    fitted, unit_match, flux_sums, curvature = lax.map(jax.vmap(one_patch), patch_ids)
    fitted = fitted.reshape(total_patches, RC, CELL, CC, CELL)
    unit_match = unit_match.reshape(total_patches, RC, CELL, CC, CELL)
    flux_sums = flux_sums.reshape(total_patches, RC * CC)
    curvature = curvature.reshape(total_patches, RC * CC)
    mean_flux = lax.optimization_barrier(jnp.mean(flux_sums.reshape(VISITS, -1), axis=1))
    mean_each = jnp.repeat(mean_flux, PATCHES * TILES)[:, None]
    correction = ((mean_each - flux_sums) / curvature).reshape(total_patches, RC, 1, CC, 1)
    matched = fitted + correction * unit_match
    matched = matched.reshape(VISITS, PATCHES, TILES, PR, PC)
    matched = jnp.transpose(matched, (0, 1, 3, 2, 4)).reshape(VISITS, NR, NC)
    return science - matched
```

```python
import numpy as np
import jax
import jax.numpy as jnp
from jax import lax
from jax.experimental import pallas as pl
from jax.experimental.pallas import tpu as pltpu
from jax.sharding import PartitionSpec as P

HALF = 15
TAPS = 2 * HALF + 1
ORDERS = 5
NBASIS = 25
CELL = 64
STAMP = 32
ROWS = 64
PAD = 16
LANES = 128
SIGMA = 5.0
MESH = pl.DeviceIdType.MESH
F32 = jnp.float32
BF16 = jnp.bfloat16


def filter_bank():
    x = (np.arange(TAPS) - HALF) / SIGMA
    env = np.exp(-0.5 * x * x)
    poly = [
        np.ones_like(x),
        2.0 * x,
        4.0 * x**2 - 2.0,
        8.0 * x**3 - 12.0 * x,
        16.0 * x**4 - 48.0 * x**2 + 12.0,
    ]
    shaped = np.stack(poly) * env[None]
    return shaped / np.sqrt(np.sum(shaped * shaped, axis=1, keepdims=True))


def taps_at(filters, index):
    inside = (index >= 0) & (index < TAPS)
    return np.where(inside[None], filters[:, np.clip(index, 0, TAPS - 1)], 0.0)


def halves(values):
    values = np.asarray(values, np.float32)
    high = values.astype(BF16)
    low = (values - high.astype(np.float32)).astype(BF16)
    return [jnp.asarray(high), jnp.asarray(low)]


def constants(filters, cells):
    width = cells * CELL
    stamp_rows = taps_at(filters, np.arange(CELL)[None, :] - np.arange(STAMP)[:, None])
    stamp_rows = stamp_rows.reshape(ORDERS * STAMP, CELL)
    one = taps_at(filters, np.arange(CELL)[:, None] - np.arange(STAMP)[None, :])
    stamp_cols = np.zeros((4, CELL, ORDERS, 4, STAMP))
    for g in range(4):
        stamp_cols[g, :, :, g, :] = np.transpose(one, (1, 0, 2))
    stamp_cols = stamp_cols.reshape(4 * CELL, ORDERS * LANES)
    full_cols = taps_at(filters, np.arange(2 * LANES)[:, None] - np.arange(LANES)[None, :] - 1)
    full_cols = np.transpose(full_cols, (1, 0, 2)).reshape(2 * LANES, ORDERS * LANES)
    full_rows = taps_at(filters, np.arange(ROWS + 2 * PAD)[None, :] - np.arange(ROWS)[:, None] - 1)
    full_rows = np.transpose(full_rows, (1, 0, 2)).reshape(ROWS, ORDERS * (ROWS + 2 * PAD))
    lane_cell = np.arange(cells * STAMP)[:, None] // STAMP == np.arange(LANES)[None, :]
    cell_lane = np.arange(LANES)[:, None] == np.arange(width)[None, :] // CELL
    return (
        halves(stamp_rows)
        + halves(stamp_cols)
        + halves(full_cols)
        + halves(full_rows)
        + [jnp.asarray(lane_cell, BF16), jnp.asarray(cell_lane, BF16)]
    )


def dot(a, b):
    return jnp.dot(a, b, preferred_element_type=F32)


def split2(x):
    high = x.astype(BF16)
    return high, (x - high.astype(F32)).astype(BF16)


def split3(x):
    high = x.astype(BF16)
    rest = x - high.astype(F32)
    mid = rest.astype(BF16)
    return high, mid, (rest - mid.astype(F32)).astype(BF16)


def dot3(a, b):
    return dot(a[0], b[0]) + (dot(a[0], b[1]) + dot(a[1], b[0]))


def pick_sum(x, selector):
    high, mid, low = split3(x)
    return dot(high, selector) + (dot(mid, selector) + dot(low, selector))


def gather_kernel(counts, owner_ref, slot_ref, out_ref, ext, landed, rs_send, rs_recv, ag_send, ag_recv, ha_send, ha_recv):
    sky_count, visits, patches = counts
    sky = lax.axis_index("sky")
    visit = lax.axis_index("visit")
    patch = lax.axis_index("patch")
    chunk = ROWS // visits
    width = slot_ref.shape[1]
    full = width + 2 * LANES
    ways = [(ds, dp) for dp in (-1, 0, 1) for ds in (-1, 0, 1) if (ds, dp) != (0, 0)]

    def exists(ds, dp):
        return (sky + ds >= 0) & (sky + ds < sky_count) & (patch + dp >= 0) & (patch + dp < patches)

    def there(ds, dp):
        return {"sky": jnp.clip(sky + ds, 0, sky_count - 1), "patch": jnp.clip(patch + dp, 0, patches - 1)}

    ext[0:PAD, :] = jnp.zeros((PAD, full), F32)
    ext[PAD + ROWS :, :] = jnp.zeros((PAD, full), F32)
    ext[PAD : PAD + ROWS, 0:LANES] = jnp.zeros((ROWS, LANES), F32)
    ext[PAD : PAD + ROWS, full - LANES :] = jnp.zeros((ROWS, LANES), F32)

    barrier = pltpu.get_barrier_semaphore()
    for d in range(1, visits):
        pl.semaphore_signal(barrier, inc=1, device_id={"visit": lax.rem(visit + d, visits)}, device_id_type=MESH)
    total = jnp.int32(visits - 1)
    for ds, dp in ways:
        ok = exists(ds, dp)

        @pl.when(ok)
        def _():
            pl.semaphore_signal(barrier, inc=1, device_id=there(ds, dp), device_id_type=MESH)

        total = total + ok.astype(jnp.int32)
    pl.semaphore_wait(barrier, total)

    scatter = []
    for d in range(1, visits):
        to = lax.rem(visit + d, visits)
        copy = pltpu.make_async_remote_copy(
            src_ref=slot_ref.at[pl.ds(pl.multiple_of(to * chunk, chunk), chunk), :],
            dst_ref=landed.at[d - 1],
            send_sem=rs_send.at[d - 1],
            recv_sem=rs_recv.at[d - 1],
            device_id={"visit": to},
            device_id_type=MESH,
        )
        copy.start()
        scatter.append(copy)
    owner = owner_ref[0, 0]
    mine = slot_ref[pl.ds(pl.multiple_of(visit * chunk, chunk), chunk), :]
    current = jnp.where(owner == visit, mine, 0.0)
    for d in range(1, visits):
        scatter[d - 1].wait_recv()
        source = lax.rem(visit + visits - d, visits)
        current = jnp.where(owner == source, landed[d - 1], current)
    here = pl.ds(pl.multiple_of(PAD + visit * chunk, chunk), chunk)
    ext[here, LANES : LANES + width] = current
    gather = []
    for d in range(1, visits):
        copy = pltpu.make_async_remote_copy(
            src_ref=ext.at[here, pl.ds(LANES, width)],
            dst_ref=ext.at[here, pl.ds(LANES, width)],
            send_sem=ag_send.at[d - 1],
            recv_sem=ag_recv.at[d - 1],
            device_id={"visit": lax.rem(visit + d, visits)},
            device_id_type=MESH,
        )
        copy.start()
        gather.append(copy)
    for d in range(1, visits):
        source = lax.rem(visit + visits - d, visits)
        rows = pl.ds(pl.multiple_of(PAD + source * chunk, chunk), chunk)
        pltpu.make_async_remote_copy(
            src_ref=ext.at[rows, pl.ds(LANES, width)],
            dst_ref=ext.at[rows, pl.ds(LANES, width)],
            send_sem=ag_send.at[d - 1],
            recv_sem=ag_recv.at[d - 1],
            device_id={"visit": source},
            device_id_type=MESH,
        ).wait_recv()

    row_span = {-1: (PAD, PAD + ROWS, PAD), 0: (PAD, PAD, ROWS), 1: (ROWS, 0, PAD)}
    col_span = {-1: (LANES, LANES + width, LANES), 0: (LANES, LANES, width), 1: (width, 0, LANES)}
    edges = []
    for way, (ds, dp) in enumerate(ways):
        row_src, row_dst, row_len = row_span[dp]
        col_src, col_dst, col_len = col_span[ds]
        copy = pltpu.make_async_remote_copy(
            src_ref=ext.at[pl.ds(row_src, row_len), pl.ds(col_src, col_len)],
            dst_ref=ext.at[pl.ds(row_dst, row_len), pl.ds(col_dst, col_len)],
            send_sem=ha_send.at[way],
            recv_sem=ha_recv.at[way],
            device_id=there(ds, dp),
            device_id_type=MESH,
        )
        edges.append(copy)

        @pl.when(exists(ds, dp))
        def _():
            copy.start()

    for copy in scatter:
        copy.wait_send()
    for copy in gather:
        copy.wait_send()
    for way, (ds, dp) in enumerate(ways):

        @pl.when(exists(ds, dp))
        def _():
            edges[way].wait_send()

        @pl.when(exists(-ds, -dp))
        def _():
            edges[way].wait_recv()

    out_ref[...] = ext[...]


def gather_coadd(owner, slot, counts):
    visits = counts[1]
    width = slot.shape[1]
    dma = pltpu.SemaphoreType.DMA
    return pl.pallas_call(
        lambda *refs: gather_kernel(counts, *refs),
        name="gather_coadd",
        out_shape=jax.ShapeDtypeStruct((ROWS + 2 * PAD, width + 2 * LANES), F32),
        in_specs=[pl.BlockSpec(memory_space=pltpu.SMEM), pl.BlockSpec(memory_space=pltpu.VMEM)],
        out_specs=pl.BlockSpec(memory_space=pltpu.VMEM),
        scratch_shapes=[
            pltpu.VMEM((ROWS + 2 * PAD, width + 2 * LANES), F32),
            pltpu.VMEM((visits - 1, ROWS // visits, width), F32),
            dma((visits - 1,)),
            dma((visits - 1,)),
            dma((visits - 1,)),
            dma((visits - 1,)),
            dma((8,)),
            dma((8,)),
        ],
        compiler_params=pltpu.CompilerParams(collective_id=0, has_side_effects=True),
    )(owner, slot)


def eliminate(rows, flux):
    count = len(rows)
    starts = [8 * (k // 8) for k in range(count)]
    for j in range(count):
        first = 8 * (j // 8)
        for i in range(j):
            if starts[i] < first:
                rows[i] = rows[i][first - starts[i] :]
                starts[i] = first
        pivot_row = rows[j]
        scaled = pivot_row * (1.0 / pivot_row[j - first : j - first + 1])
        for i in range(count):
            if i < j:
                rows[i] = rows[i] - rows[i][j - first : j - first + 1] * scaled
            elif i > j:
                factor = pivot_row[i - first : i - first + 1]
                rows[i] = rows[i] - factor * scaled[starts[i] - first :]
        rows[j] = scaled
    weights = jnp.concatenate([row[1:2] for row in rows] + [jnp.zeros((7, LANES), F32)], axis=0)
    unit = jnp.concatenate([row[2:3] for row in rows] + [jnp.zeros((7, LANES), F32)], axis=0)
    return weights, unit


def solve_kernel(
    flux, offset_ref, ext_ref, image_ref,
    srow_h, srow_l, scol_h, scol_l, fcol_h, fcol_l, frow_h, frow_l, lane_cell, cell_lane,
    resid_ref, unit_ref, rows_ref, sum_ref,
    shifted, stamps, pairs, combined_h, combined_l,
):
    width = image_ref.shape[1]
    cells = width // CELL
    full = width + 2 * LANES
    ext_rows = ROWS + 2 * PAD
    shifted[0:ext_rows, :] = pltpu.roll(ext_ref[...], full - (LANES - PAD), 1)
    shifted[ext_rows:, :] = jnp.zeros((8, full), F32)

    lane = lax.broadcasted_iota(jnp.int32, (CELL, LANES), 1)
    windows = []
    for h in range(cells // 2):
        parts = []
        for odd in range(2):
            g = 2 * h + odd
            block = shifted[:, LANES * h : LANES * h + 2 * LANES]
            block = pltpu.roll(block, ext_rows + 7 - offset_ref[0, g], 0)[0:CELL]
            move = 2 * LANES - offset_ref[1, g] - 1
            parts.append(pltpu.roll(block, move, 1)[:, 0:LANES])
        windows.append(jnp.where(lane < CELL, parts[0], parts[1]))
    window = jnp.concatenate(windows, axis=1)
    rows_done = dot3((srow_h[...], srow_l[...]), split2(window))
    groups = cells // 4
    stacked = jnp.concatenate([rows_done[:, 4 * CELL * q : 4 * CELL * (q + 1)] for q in range(groups)], axis=0)
    basis = dot3(split2(stacked), (scol_h[...], scol_l[...]))
    for q in range(groups):
        for b in range(ORDERS):
            first = (q * ORDERS + b) * STAMP
            for a in range(ORDERS):
                stamps[ORDERS * a + b, :, LANES * q : LANES * (q + 1)] = basis[first : first + STAMP, LANES * a : LANES * (a + 1)]
    lane = lax.broadcasted_iota(jnp.int32, (STAMP, LANES), 1)
    for q in range(groups):
        merged = jnp.zeros((STAMP, LANES), F32)
        for inner in range(4):
            g = 4 * q + inner
            first = LANES * (g // 2)
            block = image_ref[:, first : first + LANES]
            block = pltpu.roll(block, lax.rem(ROWS - offset_ref[0, g], ROWS), 0)[0:STAMP]
            move = lax.rem(2 * LANES + STAMP * inner - CELL * (g % 2) - offset_ref[1, g], LANES)
            merged = jnp.where(lane // STAMP == inner, pltpu.roll(block, move, 1), merged)
        stamps[NBASIS, :, LANES * q : LANES * (q + 1)] = merged
    for spare in range(NBASIS + 1, 32):
        stamps[spare] = jnp.zeros((STAMP, cells * STAMP), F32)

    spots = []
    at = 0
    for k in range(NBASIS):
        low = 8 * (k // 8)
        mine = stamps[k]
        for tile in range(low, 32, 8):
            pairs[at + tile - low : at + tile - low + 8, :] = jnp.sum(stamps[tile : tile + 8] * mine[None], axis=1)
        spots.append((at, 32 - low))
        at += 32 - low
    sums = pick_sum(pairs[...], lane_cell[...])
    rows = []
    for k, (at, length) in enumerate(spots):
        row = sums[at : at + length]
        place = lax.broadcasted_iota(jnp.int32, row.shape, 0) + (32 - length)
        row = jnp.where(place == NBASIS + 1, float(flux[k]), row)
        rows.append(row)
    padding = lax.broadcasted_iota(jnp.int32, (1, LANES), 1) >= cells
    diag = []
    for k, (at, length) in enumerate(spots):
        place = lax.broadcasted_iota(jnp.int32, rows[k].shape, 0) + (32 - length)
        diag.append(jnp.where(padding & (place == k), 1.0, rows[k]))
    weights, unit = eliminate(diag, flux)

    flux_col = jnp.concatenate([jnp.full((1, LANES), float(f), F32) for f in flux] + [jnp.zeros((7, LANES), F32)], axis=0)
    flux_cells = jnp.sum(weights * flux_col, axis=0, keepdims=True)
    curve_cells = jnp.sum(unit * flux_col, axis=0, keepdims=True)
    both = jnp.concatenate([flux_cells, curve_cells, jnp.zeros((6, LANES), F32)], axis=0)
    spread = pick_sum(jnp.concatenate([weights, unit, both], axis=0), cell_lane[...])
    rows_ref[...] = spread[64:72]
    local = jnp.sum(jnp.where(padding, 0.0, flux_cells), axis=1, keepdims=True)
    sum_ref[...] = jnp.broadcast_to(local, (8, LANES))

    blocks = width // LANES
    windows = jnp.concatenate(
        [shifted[0:ext_rows, LANES * h : LANES * h + 2 * LANES] for h in range(blocks)], axis=0
    )
    columns = dot3(split2(windows), (fcol_h[...], fcol_l[...]))
    for which in range(2):
        for h in range(blocks):
            for b in range(ORDERS):
                acc = None
                for a in range(ORDERS):
                    k = 32 * which + ORDERS * a + b
                    term = spread[k : k + 1, LANES * h : LANES * (h + 1)] * columns[
                        ext_rows * h : ext_rows * (h + 1), LANES * a : LANES * (a + 1)
                    ]
                    acc = term if acc is None else acc + term
                high, low = split2(acc)
                spot = (slice(ext_rows * b, ext_rows * (b + 1)), slice(width * which + LANES * h, width * which + LANES * (h + 1)))
                combined_h[spot] = high
                combined_l[spot] = low
    matched = dot3((frow_h[...], frow_l[...]), (combined_h[...], combined_l[...]))
    resid_ref[...] = image_ref[...] - matched[:, 0:width]
    unit_ref[...] = matched[:, width:]


def solve_cells(offsets, ext, image, filters):
    width = image.shape[1]
    cells = width // CELL
    sums = filters.sum(axis=1)
    flux = (sums[:, None] * sums[None, :]).reshape(-1)
    consts = constants(filters, cells)
    pair_rows = sum(32 - 8 * (k // 8) for k in range(NBASIS))
    vmem = pl.BlockSpec(memory_space=pltpu.VMEM)
    deep = ORDERS * (ROWS + 2 * PAD)
    return pl.pallas_call(
        lambda *refs: solve_kernel(flux, *refs),
        name="solve_cells",
        out_shape=[
            jax.ShapeDtypeStruct((ROWS, width), F32),
            jax.ShapeDtypeStruct((ROWS, width), F32),
            jax.ShapeDtypeStruct((8, width), F32),
            jax.ShapeDtypeStruct((8, LANES), F32),
        ],
        in_specs=[pl.BlockSpec(memory_space=pltpu.SMEM)] + [vmem] * (2 + len(consts)),
        out_specs=[vmem] * 4,
        scratch_shapes=[
            pltpu.VMEM((ROWS + 2 * PAD + 8, width + 2 * LANES), F32),
            pltpu.VMEM((32, STAMP, cells * STAMP), F32),
            pltpu.VMEM((pair_rows, cells * STAMP), F32),
            pltpu.VMEM((deep, 2 * width), BF16),
            pltpu.VMEM((deep, 2 * width), BF16),
        ],
        compiler_params=pltpu.CompilerParams(vmem_limit_bytes=48 << 20),
    )(offsets, ext, image, *consts)


def exchange_kernel(counts, mine_ref, out_ref, landed, send, recv):
    sky_count, _, patches = counts
    members = sky_count * patches
    me = lax.axis_index("sky") * patches + lax.axis_index("patch")

    def device(d):
        other = lax.rem(me + d, members)
        return {"sky": other // patches, "patch": lax.rem(other, patches)}

    barrier = pltpu.get_barrier_semaphore()
    for d in range(1, members):
        pl.semaphore_signal(barrier, inc=1, device_id=device(d), device_id_type=MESH)
    pl.semaphore_wait(barrier, members - 1)
    copies = []
    for d in range(1, members):
        copy = pltpu.make_async_remote_copy(
            src_ref=mine_ref,
            dst_ref=landed.at[d - 1],
            send_sem=send.at[d - 1],
            recv_sem=recv.at[d - 1],
            device_id=device(d),
            device_id_type=MESH,
        )
        copy.start()
        copies.append(copy)
    total = mine_ref[...]
    for d in range(1, members):
        copies[d - 1].wait_recv()
        total = total + landed[d - 1]
    for copy in copies:
        copy.wait_send()
    out_ref[...] = total


def exchange_sums(value, counts):
    members = counts[0] * counts[2]
    vmem = pl.BlockSpec(memory_space=pltpu.VMEM)
    return pl.pallas_call(
        lambda *refs: exchange_kernel(counts, *refs),
        name="exchange_sums",
        out_shape=jax.ShapeDtypeStruct(value.shape, F32),
        in_specs=[vmem],
        out_specs=vmem,
        scratch_shapes=[
            pltpu.VMEM((members - 1,) + value.shape, F32),
            pltpu.SemaphoreType.DMA((members - 1,)),
            pltpu.SemaphoreType.DMA((members - 1,)),
        ],
        compiler_params=pltpu.CompilerParams(collective_id=1, has_side_effects=True),
    )(value)


def solution(mesh):
    counts = (mesh.shape["sky"], mesh.shape["visit"], mesh.shape["patch"])
    filters = filter_bank()

    def body(template_store, science, owner_visit, stamp_offset):
        ext = gather_coadd(owner_visit, template_store[0], counts)
        resid, unit, rows, local = solve_cells(stamp_offset[:, 0, 0, :], ext, science[0], filters)
        total = exchange_sums(local, counts)
        stamps = science.shape[2] // CELL * counts[0] * counts[2]
        mean_flux = total[0:1, 0:1] / stamps
        correction = (mean_flux - rows[0:1]) / rows[1:2]
        return (resid - correction * unit)[None]

    spec = P("visit", "patch", "sky")
    in_specs = (spec, spec, P("sky", "patch"), P(None, "visit", "patch", "sky"))
    return jax.shard_map(body, mesh=mesh, in_specs=in_specs, out_specs=spec, check_vma=False)
```

```python
import numpy as np
import jax
import jax.numpy as jnp
from jax import lax
from jax.experimental import pallas as pl
from jax.experimental.pallas import tpu as pltpu
from jax.sharding import PartitionSpec as P

HALF = 15
TAPS = 2 * HALF + 1
ORDERS = 5
NBASIS = 25
CELL = 64
STAMP = 32
ROWS = 64
PAD = 16
LANES = 128
SIGMA = 5.0
MESH = pl.DeviceIdType.MESH
F32 = jnp.float32
BF16 = jnp.bfloat16


def filter_bank():
    x = (np.arange(TAPS) - HALF) / SIGMA
    env = np.exp(-0.5 * x * x)
    poly = [
        np.ones_like(x),
        2.0 * x,
        4.0 * x**2 - 2.0,
        8.0 * x**3 - 12.0 * x,
        16.0 * x**4 - 48.0 * x**2 + 12.0,
    ]
    shaped = np.stack(poly) * env[None]
    return shaped / np.sqrt(np.sum(shaped * shaped, axis=1, keepdims=True))


def taps_at(filters, index):
    inside = (index >= 0) & (index < TAPS)
    return np.where(inside[None], filters[:, np.clip(index, 0, TAPS - 1)], 0.0)


def halves(values):
    values = np.asarray(values, np.float32)
    high = values.astype(BF16)
    low = (values - high.astype(np.float32)).astype(BF16)
    return [jnp.asarray(np.stack([high, low]))]


def constants(filters, cells):
    width = cells * CELL
    stamp_rows = taps_at(filters, np.arange(CELL)[None, :] - np.arange(STAMP)[:, None])
    stamp_rows = stamp_rows.reshape(ORDERS * STAMP, CELL)
    one = taps_at(filters, np.arange(CELL)[:, None] - np.arange(STAMP)[None, :])
    stamp_cols = np.zeros((4, CELL, ORDERS, 4, STAMP))
    for g in range(4):
        stamp_cols[g, :, :, g, :] = np.transpose(one, (1, 0, 2))
    stamp_cols = stamp_cols.reshape(4 * CELL, ORDERS * LANES)
    full_cols = taps_at(filters, np.arange(2 * LANES)[:, None] - np.arange(LANES)[None, :] - 1)
    full_cols = np.transpose(full_cols, (1, 0, 2)).reshape(2 * LANES, ORDERS * LANES)
    full_rows = taps_at(filters, np.arange(ROWS + 2 * PAD)[None, :] - np.arange(ROWS)[:, None] - 1)
    full_rows = np.transpose(full_rows, (1, 0, 2)).reshape(ROWS, ORDERS * (ROWS + 2 * PAD))
    lane_cell = np.arange(cells * STAMP)[:, None] // STAMP == np.arange(LANES)[None, :]
    cell_lane = np.arange(LANES)[:, None] == np.arange(width)[None, :] // CELL
    return (
        halves(stamp_rows)
        + halves(stamp_cols)
        + halves(full_cols)
        + halves(full_rows)
        + [jnp.asarray(lane_cell, BF16), jnp.asarray(cell_lane, BF16)]
    )


def dot(a, b):
    return jnp.dot(a, b, preferred_element_type=F32)


def split2(x):
    high = x.astype(BF16)
    return high, (x - high.astype(F32)).astype(BF16)


def split3(x):
    high = x.astype(BF16)
    rest = x - high.astype(F32)
    mid = rest.astype(BF16)
    return high, mid, (rest - mid.astype(F32)).astype(BF16)


def dot3(a, b):
    return dot(a[0], b[0]) + (dot(a[0], b[1]) + dot(a[1], b[0]))


def pick_sum(x, selector):
    high, mid, low = split3(x)
    return dot(high, selector) + (dot(mid, selector) + dot(low, selector))


def eliminate(rows, flux):
    count = len(rows)
    starts = [8 * (k // 8) for k in range(count)]
    for j in range(count):
        first = 8 * (j // 8)
        for i in range(j):
            if starts[i] < first:
                rows[i] = rows[i][first - starts[i] :]
                starts[i] = first
        pivot_row = rows[j]
        scaled = pivot_row * (1.0 / pivot_row[j - first : j - first + 1])
        for i in range(count):
            if i < j:
                rows[i] = rows[i] - rows[i][j - first : j - first + 1] * scaled
            elif i > j:
                factor = pivot_row[i - first : i - first + 1]
                rows[i] = rows[i] - factor * scaled[starts[i] - first :]
        rows[j] = scaled
    weights = jnp.concatenate([row[1:2] for row in rows] + [jnp.zeros((7, LANES), F32)], axis=0)
    unit = jnp.concatenate([row[2:3] for row in rows] + [jnp.zeros((7, LANES), F32)], axis=0)
    return weights, unit


def fused_kernel(
    counts, flux, owner_hbm, offset_hbm, slot_hbm, image_hbm,
    srow_hbm, scol_hbm, fcol_hbm, frow_hbm, pick_hbm, put_hbm,
    out_ref,
    owner_ref, offset_ref, mine_ref, image_ref, srow, scol, fcol, frow, lane_cell, cell_lane,
    ext, landed, shifted, stamps, pairs, combined_h, combined_l, sum_ref, sum_landed,
    local_sem, rs_send, rs_recv, ag_send, ag_recv, ha_send, ha_recv, fx_send, fx_recv,
):
    sky_count, visits, patches = counts
    members = sky_count * patches
    sky = lax.axis_index("sky")
    visit = lax.axis_index("visit")
    patch = lax.axis_index("patch")
    me = sky * patches + patch
    chunk = ROWS // visits
    width = image_ref.shape[1]
    cells = width // CELL
    full = width + 2 * LANES
    ext_rows = ROWS + 2 * PAD
    ways = [(ds, dp) for dp in (-1, 0, 1) for ds in (-1, 0, 1) if (ds, dp) != (0, 0)]

    def exists(ds, dp):
        return (sky + ds >= 0) & (sky + ds < sky_count) & (patch + dp >= 0) & (patch + dp < patches)

    def there(ds, dp):
        return {"sky": jnp.clip(sky + ds, 0, sky_count - 1), "patch": jnp.clip(patch + dp, 0, patches - 1)}

    def member(d):
        other = lax.rem(me + d, members)
        return {"sky": other // patches, "patch": lax.rem(other, patches)}

    own_rows = pl.ds(pl.multiple_of(visit * chunk, chunk), chunk)
    moves = [
        (owner_hbm, owner_ref),
        (offset_hbm, offset_ref),
        (slot_hbm.at[0, own_rows, :], mine_ref),
        (image_hbm.at[0], image_ref),
        (srow_hbm, srow),
        (scol_hbm, scol),
        (fcol_hbm, fcol),
        (frow_hbm, frow),
        (pick_hbm, lane_cell),
        (put_hbm, cell_lane),
    ]
    loads = [pltpu.make_async_copy(src, dst, local_sem.at[i]) for i, (src, dst) in enumerate(moves)]

    ext[0:PAD, :] = jnp.zeros((PAD, full), F32)
    ext[PAD + ROWS :, :] = jnp.zeros((PAD, full), F32)
    ext[PAD : PAD + ROWS, 0:LANES] = jnp.zeros((ROWS, LANES), F32)
    ext[PAD : PAD + ROWS, full - LANES :] = jnp.zeros((ROWS, LANES), F32)

    barrier = pltpu.get_barrier_semaphore()
    for d in range(1, visits):
        pl.semaphore_signal(barrier, inc=1, device_id={"visit": lax.rem(visit + d, visits)}, device_id_type=MESH)
    for d in range(1, members):
        pl.semaphore_signal(barrier, inc=1, device_id=member(d), device_id_type=MESH)
    for load in loads:
        load.start()
    pl.semaphore_wait(barrier, visits - 1 + members - 1)

    scatter = []
    for d in range(1, visits):
        to = lax.rem(visit + d, visits)
        copy = pltpu.make_async_remote_copy(
            src_ref=slot_hbm.at[0, pl.ds(pl.multiple_of(to * chunk, chunk), chunk), :],
            dst_ref=landed.at[d - 1],
            send_sem=rs_send.at[d - 1],
            recv_sem=rs_recv.at[d - 1],
            device_id={"visit": to},
            device_id_type=MESH,
        )
        copy.start()
        scatter.append(copy)
    for load in loads:
        load.wait()
    groups = cells // 4
    lane = lax.broadcasted_iota(jnp.int32, (STAMP, LANES), 1)
    for q in range(groups):
        merged = jnp.zeros((STAMP, LANES), F32)
        for inner in range(4):
            g = 4 * q + inner
            first = LANES * (g // 2)
            block = image_ref[:, first : first + LANES]
            block = pltpu.roll(block, lax.rem(ROWS - offset_ref[0, 0, 0, g], ROWS), 0)[0:STAMP]
            move = lax.rem(2 * LANES + STAMP * inner - CELL * (g % 2) - offset_ref[1, 0, 0, g], LANES)
            merged = jnp.where(lane // STAMP == inner, pltpu.roll(block, move, 1), merged)
        stamps[NBASIS, :, LANES * q : LANES * (q + 1)] = merged
    for spare in range(NBASIS + 1, 32):
        stamps[spare] = jnp.zeros((STAMP, cells * STAMP), F32)

    owner = owner_ref[0, 0]
    current = jnp.where(owner == visit, mine_ref[...], 0.0)
    for d in range(1, visits):
        scatter[d - 1].wait_recv()
        source = lax.rem(visit + visits - d, visits)
        current = jnp.where(owner == source, landed[d - 1], current)
    here = pl.ds(pl.multiple_of(PAD + visit * chunk, chunk), chunk)
    ext[here, LANES : LANES + width] = current
    gather = []
    for d in range(1, visits):
        copy = pltpu.make_async_remote_copy(
            src_ref=ext.at[here, pl.ds(LANES, width)],
            dst_ref=ext.at[here, pl.ds(LANES, width)],
            send_sem=ag_send.at[d - 1],
            recv_sem=ag_recv.at[d - 1],
            device_id={"visit": lax.rem(visit + d, visits)},
            device_id_type=MESH,
        )
        copy.start()
        gather.append(copy)
    for d in range(1, visits):
        source = lax.rem(visit + visits - d, visits)
        rows = pl.ds(pl.multiple_of(PAD + source * chunk, chunk), chunk)
        pltpu.make_async_remote_copy(
            src_ref=ext.at[rows, pl.ds(LANES, width)],
            dst_ref=ext.at[rows, pl.ds(LANES, width)],
            send_sem=ag_send.at[d - 1],
            recv_sem=ag_recv.at[d - 1],
            device_id={"visit": source},
            device_id_type=MESH,
        ).wait_recv()

    row_span = {-1: (PAD, PAD + ROWS, PAD), 0: (PAD, PAD, ROWS), 1: (ROWS, 0, PAD)}
    col_span = {-1: (LANES, LANES + width, LANES), 0: (LANES, LANES, width), 1: (width, 0, LANES)}
    edges = []
    for way, (ds, dp) in enumerate(ways):
        row_src, row_dst, row_len = row_span[dp]
        col_src, col_dst, col_len = col_span[ds]
        copy = pltpu.make_async_remote_copy(
            src_ref=ext.at[pl.ds(row_src, row_len), pl.ds(col_src, col_len)],
            dst_ref=ext.at[pl.ds(row_dst, row_len), pl.ds(col_dst, col_len)],
            send_sem=ha_send.at[way],
            recv_sem=ha_recv.at[way],
            device_id=there(ds, dp),
            device_id_type=MESH,
        )
        edges.append(copy)

        @pl.when(exists(ds, dp))
        def _():
            copy.start()

    for copy in scatter:
        copy.wait_send()
    for copy in gather:
        copy.wait_send()
    for way, (ds, dp) in enumerate(ways):

        @pl.when(exists(ds, dp))
        def _():
            edges[way].wait_send()

        @pl.when(exists(-ds, -dp))
        def _():
            edges[way].wait_recv()

    shifted[0:ext_rows, :] = pltpu.roll(ext[...], full - (LANES - PAD), 1)
    shifted[ext_rows:, :] = jnp.zeros((8, full), F32)

    lane = lax.broadcasted_iota(jnp.int32, (CELL, LANES), 1)
    windows = []
    for h in range(cells // 2):
        parts = []
        for odd in range(2):
            g = 2 * h + odd
            block = shifted[:, LANES * h : LANES * h + 2 * LANES]
            block = pltpu.roll(block, ext_rows + 7 - offset_ref[0, 0, 0, g], 0)[0:CELL]
            move = 2 * LANES - offset_ref[1, 0, 0, g] - 1
            parts.append(pltpu.roll(block, move, 1)[:, 0:LANES])
        windows.append(jnp.where(lane < CELL, parts[0], parts[1]))
    window = jnp.concatenate(windows, axis=1)
    rows_done = dot3((srow[0], srow[1]), split2(window))
    stacked = jnp.concatenate([rows_done[:, 4 * CELL * q : 4 * CELL * (q + 1)] for q in range(groups)], axis=0)
    basis = dot3(split2(stacked), (scol[0], scol[1]))
    for q in range(groups):
        for b in range(ORDERS):
            first = (q * ORDERS + b) * STAMP
            for a in range(ORDERS):
                stamps[ORDERS * a + b, :, LANES * q : LANES * (q + 1)] = basis[first : first + STAMP, LANES * a : LANES * (a + 1)]
    spots = []
    at = 0
    for k in range(NBASIS):
        low = 8 * (k // 8)
        mine = stamps[k]
        for tile in range(low, 32, 8):
            pairs[at + tile - low : at + tile - low + 8, :] = jnp.sum(stamps[tile : tile + 8] * mine[None], axis=1)
        spots.append((at, 32 - low))
        at += 32 - low
    sums = pick_sum(pairs[...], lane_cell[...])
    rows = []
    for k, (at, length) in enumerate(spots):
        row = sums[at : at + length]
        place = lax.broadcasted_iota(jnp.int32, row.shape, 0) + (32 - length)
        row = jnp.where(place == NBASIS + 1, float(flux[k]), row)
        rows.append(row)
    padding = lax.broadcasted_iota(jnp.int32, (1, LANES), 1) >= cells
    diag = []
    for k, (at, length) in enumerate(spots):
        place = lax.broadcasted_iota(jnp.int32, rows[k].shape, 0) + (32 - length)
        diag.append(jnp.where(padding & (place == k), 1.0, rows[k]))
    weights, unit = eliminate(diag, flux)

    flux_col = jnp.concatenate([jnp.full((1, LANES), float(f), F32) for f in flux] + [jnp.zeros((7, LANES), F32)], axis=0)
    flux_cells = jnp.sum(weights * flux_col, axis=0, keepdims=True)
    curve_cells = jnp.sum(unit * flux_col, axis=0, keepdims=True)
    local = jnp.sum(jnp.where(padding, 0.0, flux_cells), axis=1, keepdims=True)
    sum_ref[...] = jnp.broadcast_to(local, (8, LANES))
    copies = []
    for d in range(1, members):
        copy = pltpu.make_async_remote_copy(
            src_ref=sum_ref,
            dst_ref=sum_landed.at[d - 1],
            send_sem=fx_send.at[d - 1],
            recv_sem=fx_recv.at[d - 1],
            device_id=member(d),
            device_id_type=MESH,
        )
        copy.start()
        copies.append(copy)

    both = jnp.concatenate([flux_cells, curve_cells, jnp.zeros((6, LANES), F32)], axis=0)
    spread = pick_sum(jnp.concatenate([weights, unit, both], axis=0), cell_lane[...])
    blocks = width // LANES
    windows = jnp.concatenate(
        [shifted[0:ext_rows, LANES * h : LANES * h + 2 * LANES] for h in range(blocks)], axis=0
    )
    columns = dot3(split2(windows), (fcol[0], fcol[1]))
    for which in range(2):
        for h in range(blocks):
            for b in range(ORDERS):
                acc = None
                for a in range(ORDERS):
                    k = 32 * which + ORDERS * a + b
                    term = spread[k : k + 1, LANES * h : LANES * (h + 1)] * columns[
                        ext_rows * h : ext_rows * (h + 1), LANES * a : LANES * (a + 1)
                    ]
                    acc = term if acc is None else acc + term
                high, low = split2(acc)
                spot = (slice(ext_rows * b, ext_rows * (b + 1)), slice(width * which + LANES * h, width * which + LANES * (h + 1)))
                combined_h[spot] = high
                combined_l[spot] = low
    matched = dot3((frow[0], frow[1]), (combined_h[...], combined_l[...]))
    total = sum_ref[...]
    for d in range(1, members):
        copies[d - 1].wait_recv()
        total = total + sum_landed[d - 1]
    mean_flux = total[0:1, 0:1] * (1.0 / (cells * members))
    correction = (mean_flux - spread[64:65]) / spread[65:66]
    out_ref[...] = image_ref[...] - matched[:, 0:width] - correction * matched[:, width:]
    for copy in copies:
        copy.wait_send()


def fused(owner, offsets, slot, image, filters, counts):
    width = image.shape[2]
    cells = width // CELL
    visits = counts[1]
    members = counts[0] * counts[2]
    sums = filters.sum(axis=1)
    flux = (sums[:, None] * sums[None, :]).reshape(-1)
    consts = constants(filters, cells)
    pair_rows = sum(32 - 8 * (k // 8) for k in range(NBASIS))
    deep = ORDERS * (ROWS + 2 * PAD)
    full = width + 2 * LANES
    dma = pltpu.SemaphoreType.DMA
    hbm = pl.BlockSpec(memory_space=pltpu.HBM)
    return pl.pallas_call(
        lambda *refs: fused_kernel(counts, flux, *refs),
        name="difference_patch",
        out_shape=jax.ShapeDtypeStruct((ROWS, width), F32),
        in_specs=[hbm] * (4 + len(consts)),
        out_specs=pl.BlockSpec(memory_space=pltpu.VMEM),
        scratch_shapes=[
            pltpu.SMEM(owner.shape, jnp.int32),
            pltpu.SMEM(offsets.shape, jnp.int32),
            pltpu.VMEM((ROWS // visits, width), F32),
            pltpu.VMEM((ROWS, width), F32),
        ]
        + [pltpu.VMEM(const.shape, const.dtype) for const in consts]
        + [
            pltpu.VMEM((ROWS + 2 * PAD, full), F32),
            pltpu.VMEM((visits - 1, ROWS // visits, width), F32),
            pltpu.VMEM((ROWS + 2 * PAD + 8, full), F32),
            pltpu.VMEM((32, STAMP, cells * STAMP), F32),
            pltpu.VMEM((pair_rows, cells * STAMP), F32),
            pltpu.VMEM((deep, 2 * width), BF16),
            pltpu.VMEM((deep, 2 * width), BF16),
            pltpu.VMEM((8, LANES), F32),
            pltpu.VMEM((members - 1, 8, LANES), F32),
            dma((10,)),
            dma((visits - 1,)),
            dma((visits - 1,)),
            dma((visits - 1,)),
            dma((visits - 1,)),
            dma((8,)),
            dma((8,)),
            dma((members - 1,)),
            dma((members - 1,)),
        ],
        compiler_params=pltpu.CompilerParams(
            collective_id=0, has_side_effects=True, vmem_limit_bytes=48 << 20
        ),
    )(owner, offsets, slot, image, *consts)


def solution(mesh):
    counts = (mesh.shape["sky"], mesh.shape["visit"], mesh.shape["patch"])
    filters = filter_bank()

    def body(template_store, science, owner_visit, stamp_offset):
        return fused(owner_visit, stamp_offset, template_store, science, filters, counts)[None]

    spec = P("visit", "patch", "sky")
    in_specs = (spec, spec, P("sky", "patch"), P(None, "visit", "patch", "sky"))
    return jax.shard_map(body, mesh=mesh, in_specs=in_specs, out_specs=spec, check_vma=False)
```

```python
import numpy as np
import jax
import jax.numpy as jnp
from jax import lax
from jax.experimental import pallas as pl
from jax.experimental.pallas import tpu as pltpu
from jax.sharding import PartitionSpec as P

HALF = 15
TAPS = 2 * HALF + 1
ORDERS = 5
NBASIS = 25
CELL = 64
STAMP = 32
ROWS = 64
PAD = 16
LANES = 128
SIGMA = 5.0
MESH = pl.DeviceIdType.MESH
F32 = jnp.float32
BF16 = jnp.bfloat16


def filter_bank():
    x = (np.arange(TAPS) - HALF) / SIGMA
    env = np.exp(-0.5 * x * x)
    poly = [
        np.ones_like(x),
        2.0 * x,
        4.0 * x**2 - 2.0,
        8.0 * x**3 - 12.0 * x,
        16.0 * x**4 - 48.0 * x**2 + 12.0,
    ]
    shaped = np.stack(poly) * env[None]
    return shaped / np.sqrt(np.sum(shaped * shaped, axis=1, keepdims=True))


def taps_at(filters, index):
    inside = (index >= 0) & (index < TAPS)
    return np.where(inside[None], filters[:, np.clip(index, 0, TAPS - 1)], 0.0)


def halves(values):
    values = np.asarray(values, np.float32)
    high = values.astype(BF16)
    low = (values - high.astype(np.float32)).astype(BF16)
    return [jnp.asarray(np.stack([high, low]))]


def constants(filters, cells):
    width = cells * CELL
    stamp_rows = taps_at(filters, np.arange(CELL)[None, :] - np.arange(STAMP)[:, None])
    stamp_rows = stamp_rows.reshape(ORDERS * STAMP, CELL)
    one = taps_at(filters, np.arange(CELL)[:, None] - np.arange(STAMP)[None, :])
    stamp_cols = np.zeros((4, CELL, ORDERS, 4, STAMP))
    for g in range(4):
        stamp_cols[g, :, :, g, :] = np.transpose(one, (1, 0, 2))
    stamp_cols = stamp_cols.reshape(4 * CELL, ORDERS * LANES)
    full_cols = taps_at(filters, np.arange(2 * LANES)[:, None] - np.arange(LANES)[None, :] - 1)
    full_cols = np.transpose(full_cols, (1, 0, 2)).reshape(2 * LANES, ORDERS * LANES)
    full_rows = taps_at(filters, np.arange(ROWS + 2 * PAD)[None, :] - np.arange(ROWS)[:, None] - 1)
    full_rows = np.transpose(full_rows, (1, 0, 2)).reshape(ROWS, ORDERS * (ROWS + 2 * PAD))
    lane_cell = np.arange(cells * STAMP)[:, None] // STAMP == np.arange(LANES)[None, :]
    cell_lane = np.arange(LANES)[:, None] == np.arange(width)[None, :] // CELL
    return (
        halves(stamp_rows)
        + halves(stamp_cols)
        + halves(full_cols)
        + halves(full_rows)
        + [jnp.asarray(lane_cell, BF16), jnp.asarray(cell_lane, BF16)]
    )


def dot(a, b):
    return jnp.dot(a, b, preferred_element_type=F32)


def split2(x):
    high = x.astype(BF16)
    return high, (x - high.astype(F32)).astype(BF16)


def split3(x):
    high = x.astype(BF16)
    rest = x - high.astype(F32)
    mid = rest.astype(BF16)
    return high, mid, (rest - mid.astype(F32)).astype(BF16)


def dot3(a, b):
    return dot(a[0], b[0]) + (dot(a[0], b[1]) + dot(a[1], b[0]))


def pick_sum(x, selector):
    high, mid, low = split3(x)
    return dot(high, selector) + (dot(mid, selector) + dot(low, selector))


def eliminate(rows, flux):
    count = len(rows)
    starts = [8 * (k // 8) for k in range(count)]
    for j in range(count):
        first = 8 * (j // 8)
        for i in range(j):
            if starts[i] < first:
                rows[i] = rows[i][first - starts[i] :]
                starts[i] = first
        pivot_row = rows[j]
        scaled = pivot_row * (1.0 / pivot_row[j - first : j - first + 1])
        for i in range(count):
            if i < j:
                rows[i] = rows[i] - rows[i][j - first : j - first + 1] * scaled
            elif i > j:
                factor = pivot_row[i - first : i - first + 1]
                rows[i] = rows[i] - factor * scaled[starts[i] - first :]
        rows[j] = scaled
    weights = jnp.concatenate([row[1:2] for row in rows] + [jnp.zeros((7, LANES), F32)], axis=0)
    unit = jnp.concatenate([row[2:3] for row in rows] + [jnp.zeros((7, LANES), F32)], axis=0)
    return weights, unit


def fused_kernel(
    counts, flux, owner_hbm, offset_hbm, slot_hbm, image_hbm,
    srow_hbm, scol_hbm, fcol_hbm, frow_hbm, pick_hbm, put_hbm,
    out_ref,
    owner_ref, offset_ref, mine_ref, image_ref, srow, scol, fcol, frow, lane_cell, cell_lane,
    ext, landed, shifted, stamps, pairs, combined_h, combined_l, sum_ref, sum_landed,
    local_sem, rs_send, rs_recv, ag_send, ag_recv, ha_send, ha_recv, fx_send, fx_recv,
):
    sky_count, visits, patches = counts
    members = sky_count * patches
    sky = lax.axis_index("sky")
    visit = lax.axis_index("visit")
    patch = lax.axis_index("patch")
    me = sky * patches + patch
    chunk = ROWS // visits
    width = image_ref.shape[1]
    cells = width // CELL
    full = width + 2 * LANES
    ext_rows = ROWS + 2 * PAD
    ways = [(ds, dp) for dp in (-1, 0, 1) for ds in (-1, 0, 1) if (ds, dp) != (0, 0)]

    def exists(ds, dp):
        return (sky + ds >= 0) & (sky + ds < sky_count) & (patch + dp >= 0) & (patch + dp < patches)

    def there(ds, dp):
        return {"sky": jnp.clip(sky + ds, 0, sky_count - 1), "patch": jnp.clip(patch + dp, 0, patches - 1)}

    def member(d):
        other = lax.rem(me + d, members)
        return {"sky": other // patches, "patch": lax.rem(other, patches)}

    own_rows = pl.ds(pl.multiple_of(visit * chunk, chunk), chunk)
    moves = [
        (owner_hbm, owner_ref),
        (offset_hbm, offset_ref),
        (slot_hbm.at[0, own_rows, :], mine_ref),
        (image_hbm.at[0], image_ref),
        (srow_hbm, srow),
        (scol_hbm, scol),
        (fcol_hbm, fcol),
        (frow_hbm, frow),
        (pick_hbm, lane_cell),
        (put_hbm, cell_lane),
    ]
    loads = [pltpu.make_async_copy(src, dst, local_sem.at[i]) for i, (src, dst) in enumerate(moves)]

    ext[0:PAD, :] = jnp.zeros((PAD, full), F32)
    ext[PAD + ROWS :, :] = jnp.zeros((PAD, full), F32)
    ext[PAD : PAD + ROWS, 0:LANES] = jnp.zeros((ROWS, LANES), F32)
    ext[PAD : PAD + ROWS, full - LANES :] = jnp.zeros((ROWS, LANES), F32)

    barrier = pltpu.get_barrier_semaphore()
    for d in range(1, visits):
        pl.semaphore_signal(barrier, inc=1, device_id={"visit": lax.rem(visit + d, visits)}, device_id_type=MESH)
    for d in range(1, members):
        pl.semaphore_signal(barrier, inc=1, device_id=member(d), device_id_type=MESH)
    for load in loads:
        load.start()
    pl.semaphore_wait(barrier, visits - 1 + members - 1)

    scatter = []
    for d in range(1, visits):
        to = lax.rem(visit + d, visits)
        copy = pltpu.make_async_remote_copy(
            src_ref=slot_hbm.at[0, pl.ds(pl.multiple_of(to * chunk, chunk), chunk), :],
            dst_ref=landed.at[d - 1],
            send_sem=rs_send.at[d - 1],
            recv_sem=rs_recv.at[d - 1],
            device_id={"visit": to},
            device_id_type=MESH,
        )
        copy.start()
        scatter.append(copy)
    for load in loads:
        load.wait()
    groups = cells // 4
    lane = lax.broadcasted_iota(jnp.int32, (STAMP, LANES), 1)
    for q in range(groups):
        merged = jnp.zeros((STAMP, LANES), F32)
        for inner in range(4):
            g = 4 * q + inner
            first = LANES * (g // 2)
            block = image_ref[:, first : first + LANES]
            block = pltpu.roll(block, lax.rem(ROWS - offset_ref[0, 0, 0, g], ROWS), 0)[0:STAMP]
            move = lax.rem(2 * LANES + STAMP * inner - CELL * (g % 2) - offset_ref[1, 0, 0, g], LANES)
            merged = jnp.where(lane // STAMP == inner, pltpu.roll(block, move, 1), merged)
        stamps[NBASIS, :, LANES * q : LANES * (q + 1)] = merged
    for spare in range(NBASIS + 1, 32):
        stamps[spare] = jnp.zeros((STAMP, cells * STAMP), F32)

    owner = owner_ref[0, 0]
    current = jnp.where(owner == visit, mine_ref[...], 0.0)
    for d in range(1, visits):
        scatter[d - 1].wait_recv()
        source = lax.rem(visit + visits - d, visits)
        current = jnp.where(owner == source, landed[d - 1], current)
    here = pl.ds(pl.multiple_of(PAD + visit * chunk, chunk), chunk)
    ext[here, LANES : LANES + width] = current
    gather = []
    for d in range(1, visits):
        copy = pltpu.make_async_remote_copy(
            src_ref=ext.at[here, pl.ds(LANES, width)],
            dst_ref=ext.at[here, pl.ds(LANES, width)],
            send_sem=ag_send.at[d - 1],
            recv_sem=ag_recv.at[d - 1],
            device_id={"visit": lax.rem(visit + d, visits)},
            device_id_type=MESH,
        )
        copy.start()
        gather.append(copy)
    for d in range(1, visits):
        source = lax.rem(visit + visits - d, visits)
        rows = pl.ds(pl.multiple_of(PAD + source * chunk, chunk), chunk)
        pltpu.make_async_remote_copy(
            src_ref=ext.at[rows, pl.ds(LANES, width)],
            dst_ref=ext.at[rows, pl.ds(LANES, width)],
            send_sem=ag_send.at[d - 1],
            recv_sem=ag_recv.at[d - 1],
            device_id={"visit": source},
            device_id_type=MESH,
        ).wait_recv()

    row_span = {-1: (PAD, PAD + ROWS, PAD), 0: (PAD, PAD, ROWS), 1: (ROWS, 0, PAD)}
    col_span = {-1: (LANES, LANES + width, LANES), 0: (LANES, LANES, width), 1: (width, 0, LANES)}
    edges = []
    for way, (ds, dp) in enumerate(ways):
        row_src, row_dst, row_len = row_span[dp]
        col_src, col_dst, col_len = col_span[ds]
        copy = pltpu.make_async_remote_copy(
            src_ref=ext.at[pl.ds(row_src, row_len), pl.ds(col_src, col_len)],
            dst_ref=ext.at[pl.ds(row_dst, row_len), pl.ds(col_dst, col_len)],
            send_sem=ha_send.at[way],
            recv_sem=ha_recv.at[way],
            device_id=there(ds, dp),
            device_id_type=MESH,
        )
        edges.append(copy)

        @pl.when(exists(ds, dp))
        def _():
            copy.start()

    for copy in scatter:
        copy.wait_send()
    for copy in gather:
        copy.wait_send()
    for way, (ds, dp) in enumerate(ways):

        @pl.when(exists(ds, dp))
        def _():
            edges[way].wait_send()

        @pl.when(exists(-ds, -dp))
        def _():
            edges[way].wait_recv()

    shifted[0:ext_rows, :] = pltpu.roll(ext[...], full - (LANES - PAD), 1)
    shifted[ext_rows:, :] = jnp.zeros((8, full), F32)

    lane = lax.broadcasted_iota(jnp.int32, (CELL, LANES), 1)
    windows = []
    for h in range(cells // 2):
        parts = []
        for odd in range(2):
            g = 2 * h + odd
            block = shifted[:, LANES * h : LANES * h + 2 * LANES]
            block = pltpu.roll(block, ext_rows + 7 - offset_ref[0, 0, 0, g], 0)[0:CELL]
            move = 2 * LANES - offset_ref[1, 0, 0, g] - 1
            parts.append(pltpu.roll(block, move, 1)[:, 0:LANES])
        windows.append(jnp.where(lane < CELL, parts[0], parts[1]))
    window = jnp.concatenate(windows, axis=1)
    rows_done = dot3((srow[0], srow[1]), split2(window))
    stacked = jnp.concatenate([rows_done[:, 4 * CELL * q : 4 * CELL * (q + 1)] for q in range(groups)], axis=0)
    basis = dot3(split2(stacked), (scol[0], scol[1]))
    for q in range(groups):
        for b in range(ORDERS):
            first = (q * ORDERS + b) * STAMP
            for a in range(ORDERS):
                stamps[ORDERS * a + b, :, LANES * q : LANES * (q + 1)] = basis[first : first + STAMP, LANES * a : LANES * (a + 1)]
    spots = []
    at = 0
    for k in range(NBASIS):
        low = 8 * (k // 8)
        mine = stamps[k]
        for tile in range(low, 32, 8):
            pairs[at + tile - low : at + tile - low + 8, :] = jnp.sum(stamps[tile : tile + 8] * mine[None], axis=1)
        spots.append((at, 32 - low))
        at += 32 - low
    sums = pick_sum(pairs[...], lane_cell[...])
    rows = []
    for k, (at, length) in enumerate(spots):
        row = sums[at : at + length]
        place = lax.broadcasted_iota(jnp.int32, row.shape, 0) + (32 - length)
        row = jnp.where(place == NBASIS + 1, float(flux[k]), row)
        rows.append(row)
    padding = lax.broadcasted_iota(jnp.int32, (1, LANES), 1) >= cells
    diag = []
    for k, (at, length) in enumerate(spots):
        place = lax.broadcasted_iota(jnp.int32, rows[k].shape, 0) + (32 - length)
        diag.append(jnp.where(padding & (place == k), 1.0, rows[k]))
    weights, unit = eliminate(diag, flux)

    flux_col = jnp.concatenate([jnp.full((1, LANES), float(f), F32) for f in flux] + [jnp.zeros((7, LANES), F32)], axis=0)
    flux_cells = jnp.sum(weights * flux_col, axis=0, keepdims=True)
    curve_cells = jnp.sum(unit * flux_col, axis=0, keepdims=True)
    local = jnp.sum(jnp.where(padding, 0.0, flux_cells), axis=1, keepdims=True)
    sum_ref[...] = jnp.broadcast_to(local, (8, LANES))
    copies = []
    for d in range(1, members):
        copy = pltpu.make_async_remote_copy(
            src_ref=sum_ref,
            dst_ref=sum_landed.at[d - 1],
            send_sem=fx_send.at[d - 1],
            recv_sem=fx_recv.at[d - 1],
            device_id=member(d),
            device_id_type=MESH,
        )
        copy.start()
        copies.append(copy)

    both = jnp.concatenate([flux_cells, curve_cells, jnp.zeros((6, LANES), F32)], axis=0)
    spread = pick_sum(jnp.concatenate([weights, unit, both], axis=0), cell_lane[...])
    blocks = width // LANES
    windows = jnp.concatenate(
        [shifted[0:ext_rows, LANES * h : LANES * h + 2 * LANES] for h in range(blocks)], axis=0
    )
    columns = dot3(split2(windows), (fcol[0], fcol[1]))
    for which in range(2):
        for h in range(blocks):
            for b in range(ORDERS):
                acc = None
                for a in range(ORDERS):
                    k = 32 * which + ORDERS * a + b
                    term = spread[k : k + 1, LANES * h : LANES * (h + 1)] * columns[
                        ext_rows * h : ext_rows * (h + 1), LANES * a : LANES * (a + 1)
                    ]
                    acc = term if acc is None else acc + term
                high, low = split2(acc)
                spot = (slice(ext_rows * b, ext_rows * (b + 1)), slice(width * which + LANES * h, width * which + LANES * (h + 1)))
                combined_h[spot] = high
                combined_l[spot] = low
    matched = dot3((frow[0], frow[1]), (combined_h[...], combined_l[...]))
    total = sum_ref[...]
    for d in range(1, members):
        copies[d - 1].wait_recv()
        total = total + sum_landed[d - 1]
    mean_flux = total[0:1, 0:1] * (1.0 / (cells * members))
    correction = (mean_flux - spread[64:65]) / spread[65:66]
    out_ref[...] = image_ref[...] - matched[:, 0:width] - correction * matched[:, width:]
    for copy in copies:
        copy.wait_send()


def fused(owner, offsets, slot, image, filters, counts):
    width = image.shape[2]
    cells = width // CELL
    visits = counts[1]
    members = counts[0] * counts[2]
    sums = filters.sum(axis=1)
    flux = (sums[:, None] * sums[None, :]).reshape(-1)
    consts = constants(filters, cells)
    pair_rows = sum(32 - 8 * (k // 8) for k in range(NBASIS))
    deep = ORDERS * (ROWS + 2 * PAD)
    full = width + 2 * LANES
    dma = pltpu.SemaphoreType.DMA
    hbm = pl.BlockSpec(memory_space=pltpu.HBM)
    return pl.pallas_call(
        lambda *refs: fused_kernel(counts, flux, *refs),
        name="difference_patch",
        out_shape=jax.ShapeDtypeStruct((ROWS, width), F32),
        in_specs=[hbm] * (4 + len(consts)),
        out_specs=pl.BlockSpec(memory_space=pltpu.VMEM),
        scratch_shapes=[
            pltpu.SMEM(owner.shape, jnp.int32),
            pltpu.SMEM(offsets.shape, jnp.int32),
            pltpu.VMEM((ROWS // visits, width), F32),
            pltpu.VMEM((ROWS, width), F32),
        ]
        + [pltpu.VMEM(const.shape, const.dtype) for const in consts]
        + [
            pltpu.VMEM((ROWS + 2 * PAD, full), F32),
            pltpu.VMEM((visits - 1, ROWS // visits, width), F32),
            pltpu.VMEM((ROWS + 2 * PAD + 8, full), F32),
            pltpu.VMEM((32, STAMP, cells * STAMP), F32),
            pltpu.VMEM((pair_rows, cells * STAMP), F32),
            pltpu.VMEM((deep, 2 * width), BF16),
            pltpu.VMEM((deep, 2 * width), BF16),
            pltpu.VMEM((8, LANES), F32),
            pltpu.VMEM((members - 1, 8, LANES), F32),
            dma((10,)),
            dma((visits - 1,)),
            dma((visits - 1,)),
            dma((visits - 1,)),
            dma((visits - 1,)),
            dma((8,)),
            dma((8,)),
            dma((members - 1,)),
            dma((members - 1,)),
        ],
        compiler_params=pltpu.CompilerParams(
            collective_id=0, has_side_effects=True, vmem_limit_bytes=56 << 20
        ),
    )(owner, offsets, slot, image, *consts)


def solution(mesh):
    counts = (mesh.shape["sky"], mesh.shape["visit"], mesh.shape["patch"])
    filters = filter_bank()

    def body(template_store, science, owner_visit, stamp_offset):
        return fused(owner_visit, stamp_offset, template_store, science, filters, counts)[None]

    spec = P("visit", "patch", "sky")
    in_specs = (spec, spec, P("sky", "patch"), P(None, "visit", "patch", "sky"))
    return jax.shard_map(body, mesh=mesh, in_specs=in_specs, out_specs=spec, check_vma=False)
```

```python
import numpy as np
import jax
import jax.numpy as jnp
from jax import lax
from jax.experimental import pallas as pl
from jax.experimental.pallas import tpu as pltpu
from jax.sharding import PartitionSpec as P

HALF = 15
TAPS = 2 * HALF + 1
ORDERS = 5
NBASIS = 25
CELL = 64
STAMP = 32
ROWS = 64
PAD = 16
LANES = 128
SIGMA = 5.0
MESH = pl.DeviceIdType.MESH
F32 = jnp.float32
BF16 = jnp.bfloat16


def filter_bank():
    x = (np.arange(TAPS) - HALF) / SIGMA
    env = np.exp(-0.5 * x * x)
    poly = [
        np.ones_like(x),
        2.0 * x,
        4.0 * x**2 - 2.0,
        8.0 * x**3 - 12.0 * x,
        16.0 * x**4 - 48.0 * x**2 + 12.0,
    ]
    shaped = np.stack(poly) * env[None]
    return shaped / np.sqrt(np.sum(shaped * shaped, axis=1, keepdims=True))


def taps_at(filters, index):
    inside = (index >= 0) & (index < TAPS)
    return np.where(inside[None], filters[:, np.clip(index, 0, TAPS - 1)], 0.0)


def halves(values):
    values = np.asarray(values, np.float32)
    high = values.astype(BF16)
    low = (values - high.astype(np.float32)).astype(BF16)
    return [jnp.asarray(np.stack([high, low]))]


def constants(filters, cells):
    width = cells * CELL
    stamp_rows = taps_at(filters, np.arange(CELL)[None, :] - np.arange(STAMP)[:, None])
    stamp_rows = stamp_rows.reshape(ORDERS * STAMP, CELL)
    one = taps_at(filters, np.arange(CELL)[:, None] - np.arange(STAMP)[None, :])
    stamp_cols = np.zeros((4, CELL, ORDERS, 4, STAMP))
    for g in range(4):
        stamp_cols[g, :, :, g, :] = np.transpose(one, (1, 0, 2))
    stamp_cols = stamp_cols.reshape(4 * CELL, ORDERS * LANES)
    full_cols = taps_at(filters, np.arange(2 * LANES)[:, None] - np.arange(LANES)[None, :] - 1)
    full_cols = np.transpose(full_cols, (1, 0, 2)).reshape(2 * LANES, ORDERS * LANES)
    full_rows = taps_at(filters, np.arange(ROWS + 2 * PAD)[None, :] - np.arange(ROWS)[:, None] - 1)
    full_rows = np.transpose(full_rows, (1, 0, 2)).reshape(ROWS, ORDERS * (ROWS + 2 * PAD))
    lane_cell = np.arange(cells * STAMP)[:, None] // STAMP == np.arange(LANES)[None, :]
    cell_lane = np.arange(LANES)[:, None] == np.arange(width)[None, :] // CELL
    return (
        halves(stamp_rows)
        + halves(stamp_cols)
        + halves(full_cols)
        + halves(full_rows)
        + [jnp.asarray(lane_cell, BF16), jnp.asarray(cell_lane, BF16)]
    )


def dot(a, b):
    return jnp.dot(a, b, preferred_element_type=F32)


def split2(x):
    high = x.astype(BF16)
    return high, (x - high.astype(F32)).astype(BF16)


def split3(x):
    high = x.astype(BF16)
    rest = x - high.astype(F32)
    mid = rest.astype(BF16)
    return high, mid, (rest - mid.astype(F32)).astype(BF16)


def dot3(a, b):
    return dot(a[0], b[0]) + (dot(a[0], b[1]) + dot(a[1], b[0]))


def pick_sum(x, selector):
    high, mid, low = split3(x)
    return dot(high, selector) + (dot(mid, selector) + dot(low, selector))


def eliminate(rows, flux):
    count = len(rows)
    starts = [8 * (k // 8) for k in range(count)]
    for j in range(count):
        first = 8 * (j // 8)
        for i in range(j):
            if starts[i] < first:
                rows[i] = rows[i][first - starts[i] :]
                starts[i] = first
        pivot_row = rows[j]
        scaled = pivot_row * (1.0 / pivot_row[j - first : j - first + 1])
        for i in range(count):
            if i < j:
                rows[i] = rows[i] - rows[i][j - first : j - first + 1] * scaled
            elif i > j:
                factor = pivot_row[i - first : i - first + 1]
                rows[i] = rows[i] - factor * scaled[starts[i] - first :]
        rows[j] = scaled
    weights = jnp.concatenate([row[1:2] for row in rows] + [jnp.zeros((7, LANES), F32)], axis=0)
    unit = jnp.concatenate([row[2:3] for row in rows] + [jnp.zeros((7, LANES), F32)], axis=0)
    return weights, unit


def fused_kernel(
    counts, flux, owner_hbm, offset_hbm, slot_hbm, image_hbm,
    srow_hbm, scol_hbm, fcol_hbm, frow_hbm, pick_hbm, put_hbm,
    out_ref,
    owner_ref, offset_ref, mine_ref, image_ref, srow, scol, fcol, frow, lane_cell, cell_lane,
    ext, landed, edge, edge_landed, shifted, stamps, pairs, combined_h, combined_l, sum_ref, sum_landed,
    local_sem, rs_send, rs_recv, ag_send, ag_recv, ha_send, ha_recv, fx_send, fx_recv,
):
    sky_count, visits, patches = counts
    members = sky_count * patches
    sky = lax.axis_index("sky")
    visit = lax.axis_index("visit")
    patch = lax.axis_index("patch")
    me = sky * patches + patch
    chunk = ROWS // visits
    width = image_ref.shape[1]
    cells = width // CELL
    full = width + 2 * LANES
    ext_rows = ROWS + 2 * PAD
    ways = [(ds, dp) for dp in (-1, 0, 1) for ds in (-1, 0, 1) if (ds, dp) != (0, 0)]

    def exists(ds, dp):
        return (sky + ds >= 0) & (sky + ds < sky_count) & (patch + dp >= 0) & (patch + dp < patches)

    def there(ds, dp):
        return {"sky": jnp.clip(sky + ds, 0, sky_count - 1), "patch": jnp.clip(patch + dp, 0, patches - 1)}

    def member(d):
        other = lax.rem(me + d, members)
        return {"sky": other // patches, "patch": lax.rem(other, patches)}

    own_rows = pl.ds(pl.multiple_of(visit * chunk, chunk), chunk)
    moves = [
        (owner_hbm, owner_ref),
        (offset_hbm, offset_ref),
        (slot_hbm.at[0, own_rows, :], mine_ref),
        (image_hbm.at[0], image_ref),
        (srow_hbm, srow),
        (scol_hbm, scol),
        (fcol_hbm, fcol),
        (frow_hbm, frow),
        (pick_hbm, lane_cell),
        (put_hbm, cell_lane),
    ]
    loads = [pltpu.make_async_copy(src, dst, local_sem.at[i]) for i, (src, dst) in enumerate(moves)]

    ext[0:PAD, :] = jnp.zeros((PAD, full), F32)
    ext[PAD + ROWS :, :] = jnp.zeros((PAD, full), F32)
    ext[PAD : PAD + ROWS, 0:LANES] = jnp.zeros((ROWS, LANES), F32)
    ext[PAD : PAD + ROWS, full - LANES :] = jnp.zeros((ROWS, LANES), F32)

    barrier = pltpu.get_barrier_semaphore()
    for d in range(1, visits):
        pl.semaphore_signal(barrier, inc=1, device_id={"visit": lax.rem(visit + d, visits)}, device_id_type=MESH)
    for d in range(1, members):
        pl.semaphore_signal(barrier, inc=1, device_id=member(d), device_id_type=MESH)
    for load in loads:
        load.start()
    pl.semaphore_wait(barrier, visits - 1 + members - 1)

    scatter = []
    for d in range(1, visits):
        to = lax.rem(visit + d, visits)
        copy = pltpu.make_async_remote_copy(
            src_ref=slot_hbm.at[0, pl.ds(pl.multiple_of(to * chunk, chunk), chunk), :],
            dst_ref=landed.at[d - 1],
            send_sem=rs_send.at[d - 1],
            recv_sem=rs_recv.at[d - 1],
            device_id={"visit": to},
            device_id_type=MESH,
        )
        copy.start()
        scatter.append(copy)
    for load in loads:
        load.wait()
    groups = cells // 4
    lane = lax.broadcasted_iota(jnp.int32, (STAMP, LANES), 1)
    for q in range(groups):
        merged = jnp.zeros((STAMP, LANES), F32)
        for inner in range(4):
            g = 4 * q + inner
            first = LANES * (g // 2)
            block = image_ref[:, first : first + LANES]
            block = pltpu.roll(block, lax.rem(ROWS - offset_ref[0, 0, 0, g], ROWS), 0)[0:STAMP]
            move = lax.rem(2 * LANES + STAMP * inner - CELL * (g % 2) - offset_ref[1, 0, 0, g], LANES)
            merged = jnp.where(lane // STAMP == inner, pltpu.roll(block, move, 1), merged)
        stamps[NBASIS, :, LANES * q : LANES * (q + 1)] = merged
    for spare in range(NBASIS + 1, 32):
        stamps[spare] = jnp.zeros((STAMP, cells * STAMP), F32)

    owner = owner_ref[0, 0]
    current = jnp.where(owner == visit, mine_ref[...], 0.0)
    for d in range(1, visits):
        scatter[d - 1].wait_recv()
        source = lax.rem(visit + visits - d, visits)
        current = jnp.where(owner == source, landed[d - 1], current)
    here = pl.ds(pl.multiple_of(PAD + visit * chunk, chunk), chunk)
    ext[here, LANES : LANES + width] = current
    gather = []
    for d in range(1, visits):
        copy = pltpu.make_async_remote_copy(
            src_ref=ext.at[here, pl.ds(LANES, width)],
            dst_ref=ext.at[here, pl.ds(LANES, width)],
            send_sem=ag_send.at[d - 1],
            recv_sem=ag_recv.at[d - 1],
            device_id={"visit": lax.rem(visit + d, visits)},
            device_id_type=MESH,
        )
        copy.start()
        gather.append(copy)
    for d in range(1, visits):
        source = lax.rem(visit + visits - d, visits)
        rows = pl.ds(pl.multiple_of(PAD + source * chunk, chunk), chunk)
        pltpu.make_async_remote_copy(
            src_ref=ext.at[rows, pl.ds(LANES, width)],
            dst_ref=ext.at[rows, pl.ds(LANES, width)],
            send_sem=ag_send.at[d - 1],
            recv_sem=ag_recv.at[d - 1],
            device_id={"visit": source},
            device_id_type=MESH,
        ).wait_recv()

    lane8 = lax.broadcasted_iota(jnp.int32, (8, LANES), 1) // PAD
    for side, (first, base) in enumerate(((LANES, 0), (width, LANES - PAD))):
        merged = jnp.zeros((8, LANES), F32)
        for r in range(ROWS // 8):
            block = ext[PAD + 8 * r : PAD + 8 * r + 8, first : first + LANES]
            merged = jnp.where(lane8 == r, pltpu.roll(block, (PAD * r - base) % LANES, 1), merged)
        edge[side] = merged
    row_span = {-1: (PAD, PAD + ROWS), 1: (ROWS, 0)}
    edges = []
    for way, (ds, dp) in enumerate(ways):
        if ds == 0:
            row_src, row_dst = row_span[dp]
            source = ext.at[pl.ds(row_src, PAD), pl.ds(LANES, width)]
            target = ext.at[pl.ds(row_dst, PAD), pl.ds(LANES, width)]
        else:
            source = edge.at[(ds + 1) // 2]
            target = edge_landed.at[way]
        copy = pltpu.make_async_remote_copy(
            src_ref=source,
            dst_ref=target,
            send_sem=ha_send.at[way],
            recv_sem=ha_recv.at[way],
            device_id=there(ds, dp),
            device_id_type=MESH,
        )
        edges.append(copy)

        @pl.when(exists(ds, dp))
        def _():
            copy.start()

    for copy in scatter:
        copy.wait_send()
    for copy in gather:
        copy.wait_send()
    for way, (ds, dp) in enumerate(ways):

        @pl.when(exists(-ds, -dp))
        def _():
            edges[way].wait_recv()
            if ds != 0:
                first, base = (full - LANES, 0) if ds < 0 else (0, LANES - PAD)
                spans = {0: (0, ROWS // 8, PAD), -1: (0, 2, PAD + ROWS), 1: (ROWS // 8 - 2, 2, 0)}
                group, number, row = spans[dp]
                packed = edge_landed[way]
                for r in range(number):
                    moved = pltpu.roll(packed, (base - PAD * (group + r)) % LANES, 1)
                    ext[row + 8 * r : row + 8 * r + 8, first : first + LANES] = moved

        @pl.when(exists(ds, dp))
        def _():
            edges[way].wait_send()

    shifted[0:ext_rows, :] = pltpu.roll(ext[...], full - (LANES - PAD), 1)
    shifted[ext_rows:, :] = jnp.zeros((8, full), F32)

    lane = lax.broadcasted_iota(jnp.int32, (CELL, LANES), 1)
    windows = []
    for h in range(cells // 2):
        parts = []
        for odd in range(2):
            g = 2 * h + odd
            block = shifted[:, LANES * h : LANES * h + 2 * LANES]
            block = pltpu.roll(block, ext_rows + 7 - offset_ref[0, 0, 0, g], 0)[0:CELL]
            move = 2 * LANES - offset_ref[1, 0, 0, g] - 1
            parts.append(pltpu.roll(block, move, 1)[:, 0:LANES])
        windows.append(jnp.where(lane < CELL, parts[0], parts[1]))
    window = jnp.concatenate(windows, axis=1)
    rows_done = dot3((srow[0], srow[1]), split2(window))
    stacked = jnp.concatenate([rows_done[:, 4 * CELL * q : 4 * CELL * (q + 1)] for q in range(groups)], axis=0)
    basis = dot3(split2(stacked), (scol[0], scol[1]))
    for q in range(groups):
        for b in range(ORDERS):
            first = (q * ORDERS + b) * STAMP
            for a in range(ORDERS):
                stamps[ORDERS * a + b, :, LANES * q : LANES * (q + 1)] = basis[first : first + STAMP, LANES * a : LANES * (a + 1)]
    spots = []
    at = 0
    for k in range(NBASIS):
        low = 8 * (k // 8)
        mine = stamps[k]
        for tile in range(low, 32, 8):
            pairs[at + tile - low : at + tile - low + 8, :] = jnp.sum(stamps[tile : tile + 8] * mine[None], axis=1)
        spots.append((at, 32 - low))
        at += 32 - low
    sums = pick_sum(pairs[...], lane_cell[...])
    rows = []
    for k, (at, length) in enumerate(spots):
        row = sums[at : at + length]
        place = lax.broadcasted_iota(jnp.int32, row.shape, 0) + (32 - length)
        row = jnp.where(place == NBASIS + 1, float(flux[k]), row)
        rows.append(row)
    padding = lax.broadcasted_iota(jnp.int32, (1, LANES), 1) >= cells
    diag = []
    for k, (at, length) in enumerate(spots):
        place = lax.broadcasted_iota(jnp.int32, rows[k].shape, 0) + (32 - length)
        diag.append(jnp.where(padding & (place == k), 1.0, rows[k]))
    weights, unit = eliminate(diag, flux)

    flux_col = jnp.concatenate([jnp.full((1, LANES), float(f), F32) for f in flux] + [jnp.zeros((7, LANES), F32)], axis=0)
    flux_cells = jnp.sum(weights * flux_col, axis=0, keepdims=True)
    curve_cells = jnp.sum(unit * flux_col, axis=0, keepdims=True)
    local = jnp.sum(jnp.where(padding, 0.0, flux_cells), axis=1, keepdims=True)
    sum_ref[...] = jnp.broadcast_to(local, (8, LANES))
    copies = []
    for d in range(1, members):
        copy = pltpu.make_async_remote_copy(
            src_ref=sum_ref,
            dst_ref=sum_landed.at[d - 1],
            send_sem=fx_send.at[d - 1],
            recv_sem=fx_recv.at[d - 1],
            device_id=member(d),
            device_id_type=MESH,
        )
        copy.start()
        copies.append(copy)

    both = jnp.concatenate([flux_cells, curve_cells, jnp.zeros((6, LANES), F32)], axis=0)
    spread = pick_sum(jnp.concatenate([weights, unit, both], axis=0), cell_lane[...])
    blocks = width // LANES
    windows = jnp.concatenate(
        [shifted[0:ext_rows, LANES * h : LANES * h + 2 * LANES] for h in range(blocks)], axis=0
    )
    columns = dot3(split2(windows), (fcol[0], fcol[1]))
    for which in range(2):
        for h in range(blocks):
            for b in range(ORDERS):
                acc = None
                for a in range(ORDERS):
                    k = 32 * which + ORDERS * a + b
                    term = spread[k : k + 1, LANES * h : LANES * (h + 1)] * columns[
                        ext_rows * h : ext_rows * (h + 1), LANES * a : LANES * (a + 1)
                    ]
                    acc = term if acc is None else acc + term
                high, low = split2(acc)
                spot = (slice(ext_rows * b, ext_rows * (b + 1)), slice(width * which + LANES * h, width * which + LANES * (h + 1)))
                combined_h[spot] = high
                combined_l[spot] = low
    matched = dot3((frow[0], frow[1]), (combined_h[...], combined_l[...]))
    total = sum_ref[...]
    for d in range(1, members):
        copies[d - 1].wait_recv()
        total = total + sum_landed[d - 1]
    mean_flux = total[0:1, 0:1] * (1.0 / (cells * members))
    correction = (mean_flux - spread[64:65]) / spread[65:66]
    out_ref[...] = image_ref[...] - matched[:, 0:width] - correction * matched[:, width:]
    for copy in copies:
        copy.wait_send()


def fused(owner, offsets, slot, image, filters, counts):
    width = image.shape[2]
    cells = width // CELL
    visits = counts[1]
    members = counts[0] * counts[2]
    sums = filters.sum(axis=1)
    flux = (sums[:, None] * sums[None, :]).reshape(-1)
    consts = constants(filters, cells)
    pair_rows = sum(32 - 8 * (k // 8) for k in range(NBASIS))
    deep = ORDERS * (ROWS + 2 * PAD)
    full = width + 2 * LANES
    dma = pltpu.SemaphoreType.DMA
    hbm = pl.BlockSpec(memory_space=pltpu.HBM)
    return pl.pallas_call(
        lambda *refs: fused_kernel(counts, flux, *refs),
        name="difference_patch",
        out_shape=jax.ShapeDtypeStruct((ROWS, width), F32),
        in_specs=[hbm] * (4 + len(consts)),
        out_specs=pl.BlockSpec(memory_space=pltpu.VMEM),
        scratch_shapes=[
            pltpu.SMEM(owner.shape, jnp.int32),
            pltpu.SMEM(offsets.shape, jnp.int32),
            pltpu.VMEM((ROWS // visits, width), F32),
            pltpu.VMEM((ROWS, width), F32),
        ]
        + [pltpu.VMEM(const.shape, const.dtype) for const in consts]
        + [
            pltpu.VMEM((ROWS + 2 * PAD, full), F32),
            pltpu.VMEM((visits - 1, ROWS // visits, width), F32),
            pltpu.VMEM((2, 8, LANES), F32),
            pltpu.VMEM((8, 8, LANES), F32),
            pltpu.VMEM((ROWS + 2 * PAD + 8, full), F32),
            pltpu.VMEM((32, STAMP, cells * STAMP), F32),
            pltpu.VMEM((pair_rows, cells * STAMP), F32),
            pltpu.VMEM((deep, 2 * width), BF16),
            pltpu.VMEM((deep, 2 * width), BF16),
            pltpu.VMEM((8, LANES), F32),
            pltpu.VMEM((members - 1, 8, LANES), F32),
            dma((10,)),
            dma((visits - 1,)),
            dma((visits - 1,)),
            dma((visits - 1,)),
            dma((visits - 1,)),
            dma((8,)),
            dma((8,)),
            dma((members - 1,)),
            dma((members - 1,)),
        ],
        compiler_params=pltpu.CompilerParams(
            collective_id=0, has_side_effects=True, vmem_limit_bytes=56 << 20
        ),
    )(owner, offsets, slot, image, *consts)


def solution(mesh):
    counts = (mesh.shape["sky"], mesh.shape["visit"], mesh.shape["patch"])
    filters = filter_bank()

    def body(template_store, science, owner_visit, stamp_offset):
        return fused(owner_visit, stamp_offset, template_store, science, filters, counts)[None]

    spec = P("visit", "patch", "sky")
    in_specs = (spec, spec, P("sky", "patch"), P(None, "visit", "patch", "sky"))
    return jax.shard_map(body, mesh=mesh, in_specs=in_specs, out_specs=spec, check_vma=False)
```

```python
import numpy as np
import jax
import jax.numpy as jnp
from jax import lax
from jax.experimental import pallas as pl
from jax.experimental.pallas import tpu as pltpu
from jax.sharding import PartitionSpec as P

HALF = 15
TAPS = 2 * HALF + 1
ORDERS = 5
NBASIS = 25
CELL = 64
STAMP = 32
ROWS = 64
PAD = 16
LANES = 128
SIGMA = 5.0
MESH = pl.DeviceIdType.MESH
F32 = jnp.float32
BF16 = jnp.bfloat16


def filter_bank():
    x = (np.arange(TAPS) - HALF) / SIGMA
    env = np.exp(-0.5 * x * x)
    poly = [
        np.ones_like(x),
        2.0 * x,
        4.0 * x**2 - 2.0,
        8.0 * x**3 - 12.0 * x,
        16.0 * x**4 - 48.0 * x**2 + 12.0,
    ]
    shaped = np.stack(poly) * env[None]
    return shaped / np.sqrt(np.sum(shaped * shaped, axis=1, keepdims=True))


def taps_at(filters, index):
    inside = (index >= 0) & (index < TAPS)
    return np.where(inside[None], filters[:, np.clip(index, 0, TAPS - 1)], 0.0)


def halves(values):
    values = np.asarray(values, np.float32)
    high = values.astype(BF16)
    low = (values - high.astype(np.float32)).astype(BF16)
    return [jnp.asarray(np.stack([high, low]))]


def constants(filters, cells):
    width = cells * CELL
    stamp_rows = taps_at(filters, np.arange(CELL)[None, :] - np.arange(STAMP)[:, None])
    stamp_rows = stamp_rows.reshape(ORDERS * STAMP, CELL)
    one = taps_at(filters, np.arange(CELL)[:, None] - np.arange(STAMP)[None, :])
    stamp_cols = np.zeros((4, CELL, ORDERS, 4, STAMP))
    for g in range(4):
        stamp_cols[g, :, :, g, :] = np.transpose(one, (1, 0, 2))
    stamp_cols = stamp_cols.reshape(4 * CELL, ORDERS * LANES)
    full_cols = taps_at(filters, np.arange(2 * LANES)[:, None] - np.arange(LANES)[None, :] - 1)
    full_cols = np.transpose(full_cols, (1, 0, 2)).reshape(2 * LANES, ORDERS * LANES)
    full_rows = taps_at(filters, np.arange(ROWS + 2 * PAD)[None, :] - np.arange(ROWS)[:, None] - 1)
    full_rows = np.transpose(full_rows, (1, 0, 2)).reshape(ROWS, ORDERS * (ROWS + 2 * PAD))
    lane_cell = np.arange(cells * STAMP)[:, None] // STAMP == np.arange(LANES)[None, :]
    cell_lane = np.arange(LANES)[:, None] == np.arange(width)[None, :] // CELL
    return (
        halves(stamp_rows)
        + halves(stamp_cols)
        + halves(full_cols)
        + halves(full_rows)
        + [jnp.asarray(lane_cell, BF16), jnp.asarray(cell_lane, BF16)]
    )


def dot(a, b):
    return jnp.dot(a, b, preferred_element_type=F32)


def split2(x):
    high = x.astype(BF16)
    return high, (x - high.astype(F32)).astype(BF16)


def split3(x):
    high = x.astype(BF16)
    rest = x - high.astype(F32)
    mid = rest.astype(BF16)
    return high, mid, (rest - mid.astype(F32)).astype(BF16)


def dot3(a, b):
    return dot(a[0], b[0]) + (dot(a[0], b[1]) + dot(a[1], b[0]))


def pick_sum(x, selector):
    high, mid, low = split3(x)
    return dot(high, selector) + (dot(mid, selector) + dot(low, selector))


def eliminate(rows, flux):
    count = len(rows)
    starts = [8 * (k // 8) for k in range(count)]
    for j in range(count):
        first = 8 * (j // 8)
        for i in range(j):
            if starts[i] < first:
                rows[i] = rows[i][first - starts[i] :]
                starts[i] = first
        pivot_row = rows[j]
        scaled = pivot_row * (1.0 / pivot_row[j - first : j - first + 1])
        for i in range(count):
            if i < j:
                rows[i] = rows[i] - rows[i][j - first : j - first + 1] * scaled
            elif i > j:
                factor = pivot_row[i - first : i - first + 1]
                rows[i] = rows[i] - factor * scaled[starts[i] - first :]
        rows[j] = scaled
    weights = jnp.concatenate([row[1:2] for row in rows] + [jnp.zeros((7, LANES), F32)], axis=0)
    unit = jnp.concatenate([row[2:3] for row in rows] + [jnp.zeros((7, LANES), F32)], axis=0)
    return weights, unit


def fused_kernel(
    counts, flux, owner_hbm, offset_hbm, slot_hbm, image_hbm,
    srow_hbm, scol_hbm, fcol_hbm, frow_hbm, pick_hbm, put_hbm,
    out_ref,
    owner_ref, offset_ref, mine_ref, image_ref, srow, scol, fcol, frow, lane_cell, cell_lane,
    ext, landed, edge, edge_landed, shifted, stamps, pairs, combined_h, combined_l, sum_ref, sum_landed,
    local_sem, rs_send, rs_recv, ag_send, ag_recv, ha_send, ha_recv, fx_send, fx_recv,
):
    sky_count, visits, patches = counts
    members = sky_count * patches
    sky = lax.axis_index("sky")
    visit = lax.axis_index("visit")
    patch = lax.axis_index("patch")
    me = sky * patches + patch
    chunk = ROWS // visits
    width = image_ref.shape[1]
    cells = width // CELL
    full = width + 2 * LANES
    ext_rows = ROWS + 2 * PAD
    ways = [(ds, dp) for dp in (-1, 0, 1) for ds in (-1, 0, 1) if (ds, dp) != (0, 0)]

    def exists(ds, dp):
        return (sky + ds >= 0) & (sky + ds < sky_count) & (patch + dp >= 0) & (patch + dp < patches)

    def there(ds, dp):
        return {"sky": jnp.clip(sky + ds, 0, sky_count - 1), "patch": jnp.clip(patch + dp, 0, patches - 1)}

    def member(d):
        other = lax.rem(me + d, members)
        return {"sky": other // patches, "patch": lax.rem(other, patches)}

    own_rows = pl.ds(pl.multiple_of(visit * chunk, chunk), chunk)
    moves = [
        (owner_hbm, owner_ref),
        (offset_hbm, offset_ref),
        (slot_hbm.at[0, own_rows, :], mine_ref),
        (image_hbm.at[0], image_ref),
        (srow_hbm, srow),
        (scol_hbm, scol),
        (fcol_hbm, fcol),
        (frow_hbm, frow),
        (pick_hbm, lane_cell),
        (put_hbm, cell_lane),
    ]
    loads = [pltpu.make_async_copy(src, dst, local_sem.at[i]) for i, (src, dst) in enumerate(moves)]

    ext[0:PAD, :] = jnp.zeros((PAD, full), F32)
    ext[PAD + ROWS :, :] = jnp.zeros((PAD, full), F32)
    ext[PAD : PAD + ROWS, 0:LANES] = jnp.zeros((ROWS, LANES), F32)
    ext[PAD : PAD + ROWS, full - LANES :] = jnp.zeros((ROWS, LANES), F32)

    barrier = pltpu.get_barrier_semaphore()
    for d in range(1, visits):
        pl.semaphore_signal(barrier, inc=1, device_id={"visit": lax.rem(visit + d, visits)}, device_id_type=MESH)
    for d in range(1, members):
        pl.semaphore_signal(barrier, inc=1, device_id=member(d), device_id_type=MESH)
    for load in loads:
        load.start()
    pl.semaphore_wait(barrier, visits - 1 + members - 1)

    scatter = []
    for d in range(1, visits):
        to = lax.rem(visit + d, visits)
        copy = pltpu.make_async_remote_copy(
            src_ref=slot_hbm.at[0, pl.ds(pl.multiple_of(to * chunk, chunk), chunk), :],
            dst_ref=landed.at[d - 1],
            send_sem=rs_send.at[d - 1],
            recv_sem=rs_recv.at[d - 1],
            device_id={"visit": to},
            device_id_type=MESH,
        )
        copy.start()
        scatter.append(copy)
    for load in loads:
        load.wait()
    groups = cells // 4
    lane = lax.broadcasted_iota(jnp.int32, (STAMP, LANES), 1)
    for q in range(groups):
        merged = jnp.zeros((STAMP, LANES), F32)
        for inner in range(4):
            g = 4 * q + inner
            first = LANES * (g // 2)
            block = image_ref[:, first : first + LANES]
            block = pltpu.roll(block, lax.rem(ROWS - offset_ref[0, 0, 0, g], ROWS), 0)[0:STAMP]
            move = lax.rem(2 * LANES + STAMP * inner - CELL * (g % 2) - offset_ref[1, 0, 0, g], LANES)
            merged = jnp.where(lane // STAMP == inner, pltpu.roll(block, move, 1), merged)
        stamps[NBASIS, :, LANES * q : LANES * (q + 1)] = merged
    for spare in range(NBASIS + 1, 32):
        stamps[spare] = jnp.zeros((STAMP, cells * STAMP), F32)

    owner = owner_ref[0, 0]
    current = jnp.where(owner == visit, mine_ref[...], 0.0)
    for d in range(1, visits):
        scatter[d - 1].wait_recv()
        source = lax.rem(visit + visits - d, visits)
        current = jnp.where(owner == source, landed[d - 1], current)
    here = pl.ds(pl.multiple_of(PAD + visit * chunk, chunk), chunk)
    ext[here, LANES : LANES + width] = current
    gather = []
    for d in range(1, visits):
        copy = pltpu.make_async_remote_copy(
            src_ref=ext.at[here, pl.ds(LANES, width)],
            dst_ref=ext.at[here, pl.ds(LANES, width)],
            send_sem=ag_send.at[d - 1],
            recv_sem=ag_recv.at[d - 1],
            device_id={"visit": lax.rem(visit + d, visits)},
            device_id_type=MESH,
        )
        copy.start()
        gather.append(copy)
    for d in range(1, visits):
        source = lax.rem(visit + visits - d, visits)
        rows = pl.ds(pl.multiple_of(PAD + source * chunk, chunk), chunk)
        pltpu.make_async_remote_copy(
            src_ref=ext.at[rows, pl.ds(LANES, width)],
            dst_ref=ext.at[rows, pl.ds(LANES, width)],
            send_sem=ag_send.at[d - 1],
            recv_sem=ag_recv.at[d - 1],
            device_id={"visit": source},
            device_id_type=MESH,
        ).wait_recv()

    lane8 = lax.broadcasted_iota(jnp.int32, (8, LANES), 1) // PAD
    for side, (first, base) in enumerate(((LANES, 0), (width, LANES - PAD))):
        merged = jnp.zeros((8, LANES), F32)
        for r in range(ROWS // 8):
            block = ext[PAD + 8 * r : PAD + 8 * r + 8, first : first + LANES]
            merged = jnp.where(lane8 == r, pltpu.roll(block, (PAD * r - base) % LANES, 1), merged)
        edge[side] = merged
    row_span = {-1: (PAD, PAD + ROWS), 1: (ROWS, 0)}
    edges = []
    for way, (ds, dp) in enumerate(ways):
        if ds == 0:
            row_src, row_dst = row_span[dp]
            source = ext.at[pl.ds(row_src, PAD), pl.ds(LANES, width)]
            target = ext.at[pl.ds(row_dst, PAD), pl.ds(LANES, width)]
        else:
            source = edge.at[(ds + 1) // 2]
            target = edge_landed.at[way]
        copy = pltpu.make_async_remote_copy(
            src_ref=source,
            dst_ref=target,
            send_sem=ha_send.at[way],
            recv_sem=ha_recv.at[way],
            device_id=there(ds, dp),
            device_id_type=MESH,
        )
        edges.append(copy)

        @pl.when(exists(ds, dp))
        def _():
            copy.start()

    for copy in scatter:
        copy.wait_send()
    for copy in gather:
        copy.wait_send()
    for way, (ds, dp) in enumerate(ways):

        @pl.when(exists(-ds, -dp))
        def _():
            edges[way].wait_recv()
            if ds != 0:
                first, base = (full - LANES, 0) if ds < 0 else (0, LANES - PAD)
                spans = {0: (0, ROWS // 8, PAD), -1: (0, 2, PAD + ROWS), 1: (ROWS // 8 - 2, 2, 0)}
                group, number, row = spans[dp]
                packed = edge_landed[way]
                for r in range(number):
                    moved = pltpu.roll(packed, (base - PAD * (group + r)) % LANES, 1)
                    ext[row + 8 * r : row + 8 * r + 8, first : first + LANES] = moved

        @pl.when(exists(ds, dp))
        def _():
            edges[way].wait_send()

    shifted[0:ext_rows, :] = pltpu.roll(ext[...], full - (LANES - PAD), 1)
    shifted[ext_rows:, :] = jnp.zeros((8, full), F32)

    lane = lax.broadcasted_iota(jnp.int32, (CELL, LANES), 1)
    windows = []
    for h in range(cells // 2):
        parts = []
        for odd in range(2):
            g = 2 * h + odd
            block = shifted[:, LANES * h : LANES * h + 2 * LANES]
            block = pltpu.roll(block, ext_rows + 7 - offset_ref[0, 0, 0, g], 0)[0:CELL]
            move = 2 * LANES - offset_ref[1, 0, 0, g] - 1
            parts.append(pltpu.roll(block, move, 1)[:, 0:LANES])
        windows.append(jnp.where(lane < CELL, parts[0], parts[1]))
    window = jnp.concatenate(windows, axis=1)
    rows_done = dot3((srow[0], srow[1]), split2(window))
    stacked = jnp.concatenate([rows_done[:, 4 * CELL * q : 4 * CELL * (q + 1)] for q in range(groups)], axis=0)
    basis = dot3(split2(stacked), (scol[0], scol[1]))
    for q in range(groups):
        for b in range(ORDERS):
            first = (q * ORDERS + b) * STAMP
            for a in range(ORDERS):
                stamps[ORDERS * a + b, :, LANES * q : LANES * (q + 1)] = basis[first : first + STAMP, LANES * a : LANES * (a + 1)]
    spots = []
    at = 0
    for k in range(NBASIS):
        low = 8 * (k // 8)
        mine = stamps[k]
        for tile in range(low, 32, 8):
            pairs[at + tile - low : at + tile - low + 8, :] = jnp.sum(stamps[tile : tile + 8] * mine[None], axis=1)
        spots.append((at, 32 - low))
        at += 32 - low
    sums = pick_sum(pairs[...], lane_cell[...])
    rows = []
    for k, (at, length) in enumerate(spots):
        row = sums[at : at + length]
        place = lax.broadcasted_iota(jnp.int32, row.shape, 0) + (32 - length)
        row = jnp.where(place == NBASIS + 1, float(flux[k]), row)
        rows.append(row)
    padding = lax.broadcasted_iota(jnp.int32, (1, LANES), 1) >= cells
    diag = []
    for k, (at, length) in enumerate(spots):
        place = lax.broadcasted_iota(jnp.int32, rows[k].shape, 0) + (32 - length)
        diag.append(jnp.where(padding & (place == k), 1.0, rows[k]))
    weights, unit = eliminate(diag, flux)

    flux_col = jnp.concatenate([jnp.full((1, LANES), float(f), F32) for f in flux] + [jnp.zeros((7, LANES), F32)], axis=0)
    flux_cells = jnp.sum(weights * flux_col, axis=0, keepdims=True)
    curve_cells = jnp.sum(unit * flux_col, axis=0, keepdims=True)
    local = jnp.sum(jnp.where(padding, 0.0, flux_cells), axis=1, keepdims=True)
    sum_ref[...] = jnp.broadcast_to(local, (8, LANES))
    copies = []
    for d in range(1, members):
        copy = pltpu.make_async_remote_copy(
            src_ref=sum_ref,
            dst_ref=sum_landed.at[d - 1],
            send_sem=fx_send.at[d - 1],
            recv_sem=fx_recv.at[d - 1],
            device_id=member(d),
            device_id_type=MESH,
        )
        copy.start()
        copies.append(copy)

    both = jnp.concatenate([flux_cells, curve_cells, jnp.zeros((6, LANES), F32)], axis=0)
    spread = pick_sum(jnp.concatenate([weights, unit, both], axis=0), cell_lane[...])
    blocks = width // LANES
    windows = jnp.concatenate(
        [shifted[0:ext_rows, LANES * h : LANES * h + 2 * LANES] for h in range(blocks)], axis=0
    )
    columns = dot3(split2(windows), (fcol[0], fcol[1]))
    for which in range(2):
        for h in range(blocks):
            for b in range(ORDERS):
                acc = None
                for a in range(ORDERS):
                    k = 32 * which + ORDERS * a + b
                    term = spread[k : k + 1, LANES * h : LANES * (h + 1)] * columns[
                        ext_rows * h : ext_rows * (h + 1), LANES * a : LANES * (a + 1)
                    ]
                    acc = term if acc is None else acc + term
                high, low = split2(acc)
                spot = (slice(ext_rows * b, ext_rows * (b + 1)), slice(width * which + LANES * h, width * which + LANES * (h + 1)))
                combined_h[spot] = high
                combined_l[spot] = low
    matched = dot3((frow[0], frow[1]), (combined_h[...], combined_l[...]))
    total = sum_ref[...]
    for d in range(1, members):
        copies[d - 1].wait_recv()
        total = total + sum_landed[d - 1]
    mean_flux = total[0:1, 0:1] * (1.0 / (cells * members))
    correction = (mean_flux - spread[64:65]) / spread[65:66]
    out_ref[...] = image_ref[...] - matched[:, 0:width] - correction * matched[:, width:]
    for copy in copies:
        copy.wait_send()


def fused(owner, offsets, slot, image, filters, counts):
    width = image.shape[2]
    cells = width // CELL
    visits = counts[1]
    members = counts[0] * counts[2]
    sums = filters.sum(axis=1)
    flux = (sums[:, None] * sums[None, :]).reshape(-1)
    consts = constants(filters, cells)
    pair_rows = sum(32 - 8 * (k // 8) for k in range(NBASIS))
    deep = ORDERS * (ROWS + 2 * PAD)
    full = width + 2 * LANES
    dma = pltpu.SemaphoreType.DMA
    hbm = pl.BlockSpec(memory_space=pltpu.HBM)
    return pl.pallas_call(
        lambda *refs: fused_kernel(counts, flux, *refs),
        name="difference_patch",
        out_shape=jax.ShapeDtypeStruct((ROWS, width), F32),
        in_specs=[hbm] * (4 + len(consts)),
        out_specs=pl.BlockSpec(memory_space=pltpu.VMEM),
        scratch_shapes=[
            pltpu.SMEM(owner.shape, jnp.int32),
            pltpu.SMEM(offsets.shape, jnp.int32),
            pltpu.VMEM((ROWS // visits, width), F32),
            pltpu.VMEM((ROWS, width), F32),
        ]
        + [pltpu.VMEM(const.shape, const.dtype) for const in consts]
        + [
            pltpu.VMEM((ROWS + 2 * PAD, full), F32),
            pltpu.VMEM((visits - 1, ROWS // visits, width), F32),
            pltpu.VMEM((2, 8, LANES), F32),
            pltpu.VMEM((8, 8, LANES), F32),
            pltpu.VMEM((ROWS + 2 * PAD + 8, full), F32),
            pltpu.VMEM((32, STAMP, cells * STAMP), F32),
            pltpu.VMEM((pair_rows, cells * STAMP), F32),
            pltpu.VMEM((deep, 2 * width), BF16),
            pltpu.VMEM((deep, 2 * width), BF16),
            pltpu.VMEM((8, LANES), F32),
            pltpu.VMEM((members - 1, 8, LANES), F32),
            dma((10,)),
            dma((visits - 1,)),
            dma((visits - 1,)),
            dma((visits - 1,)),
            dma((visits - 1,)),
            dma((8,)),
            dma((8,)),
            dma((members - 1,)),
            dma((members - 1,)),
        ],
        compiler_params=pltpu.CompilerParams(
            collective_id=0, has_side_effects=True, vmem_limit_bytes=40 << 20
        ),
    )(owner, *[pltpu.with_memory_space_constraint(v, pltpu.HBM) for v in (offsets, slot, image, *consts)])


def solution(mesh):
    counts = (mesh.shape["sky"], mesh.shape["visit"], mesh.shape["patch"])
    filters = filter_bank()

    def body(template_store, science, owner_visit, stamp_offset):
        return fused(owner_visit, stamp_offset, template_store, science, filters, counts)[None]

    spec = P("visit", "patch", "sky")
    in_specs = (spec, spec, P("sky", "patch"), P(None, "visit", "patch", "sky"))
    return jax.shard_map(body, mesh=mesh, in_specs=in_specs, out_specs=spec, check_vma=False)
```

```python
import numpy as np
import jax
import jax.numpy as jnp
from jax import lax
from jax.experimental import pallas as pl
from jax.experimental.pallas import tpu as pltpu
from jax.sharding import PartitionSpec as P

HALF = 15
TAPS = 2 * HALF + 1
ORDERS = 5
NBASIS = 25
CELL = 64
STAMP = 32
ROWS = 64
PAD = 16
LANES = 128
SIGMA = 5.0
MESH = pl.DeviceIdType.MESH
F32 = jnp.float32
BF16 = jnp.bfloat16


def filter_bank():
    x = (np.arange(TAPS) - HALF) / SIGMA
    env = np.exp(-0.5 * x * x)
    poly = [
        np.ones_like(x),
        2.0 * x,
        4.0 * x**2 - 2.0,
        8.0 * x**3 - 12.0 * x,
        16.0 * x**4 - 48.0 * x**2 + 12.0,
    ]
    shaped = np.stack(poly) * env[None]
    return shaped / np.sqrt(np.sum(shaped * shaped, axis=1, keepdims=True))


def taps_at(filters, index):
    inside = (index >= 0) & (index < TAPS)
    return np.where(inside[None], filters[:, np.clip(index, 0, TAPS - 1)], 0.0)


def halves(values):
    values = np.asarray(values, np.float32)
    high = values.astype(BF16)
    low = (values - high.astype(np.float32)).astype(BF16)
    return [jnp.asarray(np.stack([high, low]))]


def constants(filters, cells):
    width = cells * CELL
    stamp_rows = taps_at(filters, np.arange(CELL)[None, :] - np.arange(STAMP)[:, None])
    stamp_rows = stamp_rows.reshape(ORDERS * STAMP, CELL)
    one = taps_at(filters, np.arange(CELL)[:, None] - np.arange(STAMP)[None, :])
    stamp_cols = np.zeros((4, CELL, ORDERS, 4, STAMP))
    for g in range(4):
        stamp_cols[g, :, :, g, :] = np.transpose(one, (1, 0, 2))
    stamp_cols = stamp_cols.reshape(4 * CELL, ORDERS * LANES)
    full_cols = taps_at(filters, np.arange(2 * LANES)[:, None] - np.arange(LANES)[None, :] - 1)
    full_cols = np.transpose(full_cols, (1, 0, 2)).reshape(2 * LANES, ORDERS * LANES)
    full_rows = taps_at(filters, np.arange(ROWS + 2 * PAD)[None, :] - np.arange(ROWS)[:, None] - 1)
    full_rows = np.transpose(full_rows, (1, 0, 2)).reshape(ROWS, ORDERS * (ROWS + 2 * PAD))
    lane_cell = np.arange(cells * STAMP)[:, None] // STAMP == np.arange(LANES)[None, :]
    cell_lane = np.arange(LANES)[:, None] == np.arange(width)[None, :] // CELL
    return (
        halves(stamp_rows)
        + halves(stamp_cols)
        + halves(full_cols)
        + halves(full_rows)
        + [jnp.asarray(lane_cell, BF16), jnp.asarray(cell_lane, BF16)]
    )


def dot(a, b):
    return jnp.dot(a, b, preferred_element_type=F32)


def split2(x):
    high = x.astype(BF16)
    return high, (x - high.astype(F32)).astype(BF16)


def split3(x):
    high = x.astype(BF16)
    rest = x - high.astype(F32)
    mid = rest.astype(BF16)
    return high, mid, (rest - mid.astype(F32)).astype(BF16)


def dot3(a, b):
    return dot(a[0], b[0]) + (dot(a[0], b[1]) + dot(a[1], b[0]))


def pick_sum(x, selector):
    high, mid, low = split3(x)
    return dot(high, selector) + (dot(mid, selector) + dot(low, selector))


def eliminate(rows, flux):
    count = len(rows)
    starts = [8 * (k // 8) for k in range(count)]
    for j in range(count):
        first = 8 * (j // 8)
        for i in range(j):
            if starts[i] < first:
                rows[i] = rows[i][first - starts[i] :]
                starts[i] = first
        pivot_row = rows[j]
        scaled = pivot_row * (1.0 / pivot_row[j - first : j - first + 1])
        for i in range(count):
            if i < j:
                rows[i] = rows[i] - rows[i][j - first : j - first + 1] * scaled
            elif i > j:
                factor = pivot_row[i - first : i - first + 1]
                rows[i] = rows[i] - factor * scaled[starts[i] - first :]
        rows[j] = scaled
    weights = jnp.concatenate([row[1:2] for row in rows] + [jnp.zeros((7, LANES), F32)], axis=0)
    unit = jnp.concatenate([row[2:3] for row in rows] + [jnp.zeros((7, LANES), F32)], axis=0)
    return weights, unit


def fused_kernel(
    counts, flux, owner_hbm, offset_hbm, slot_hbm, image_hbm,
    srow_hbm, scol_hbm, fcol_hbm, frow_hbm, pick_hbm, put_hbm,
    out_ref,
    owner_ref, offset_ref, slot_ref, image_ref, srow, scol, fcol, frow, lane_cell, cell_lane,
    ext, landed, edge, edge_landed, shifted, stamps, pairs, combined_h, combined_l, sum_ref, sum_landed,
    local_sem, rs_send, rs_recv, ag_send, ag_recv, ha_send, ha_recv, fx_send, fx_recv,
):
    sky_count, visits, patches = counts
    members = sky_count * patches
    sky = lax.axis_index("sky")
    visit = lax.axis_index("visit")
    patch = lax.axis_index("patch")
    me = sky * patches + patch
    chunk = ROWS // visits
    width = image_ref.shape[1]
    cells = width // CELL
    full = width + 2 * LANES
    ext_rows = ROWS + 2 * PAD
    ways = [(ds, dp) for dp in (-1, 0, 1) for ds in (-1, 0, 1) if (ds, dp) != (0, 0)]

    def exists(ds, dp):
        return (sky + ds >= 0) & (sky + ds < sky_count) & (patch + dp >= 0) & (patch + dp < patches)

    def there(ds, dp):
        return {"sky": jnp.clip(sky + ds, 0, sky_count - 1), "patch": jnp.clip(patch + dp, 0, patches - 1)}

    def member(d):
        other = lax.rem(me + d, members)
        return {"sky": other // patches, "patch": lax.rem(other, patches)}

    own_rows = pl.ds(pl.multiple_of(visit * chunk, chunk), chunk)
    moves = [
        (slot_hbm.at[0], slot_ref),
        (owner_hbm, owner_ref),
        (offset_hbm, offset_ref),
        (image_hbm.at[0], image_ref),
        (srow_hbm, srow),
        (scol_hbm, scol),
        (fcol_hbm, fcol),
        (frow_hbm, frow),
        (pick_hbm, lane_cell),
        (put_hbm, cell_lane),
    ]
    loads = [pltpu.make_async_copy(src, dst, local_sem.at[i]) for i, (src, dst) in enumerate(moves)]

    ext[0:PAD, :] = jnp.zeros((PAD, full), F32)
    ext[PAD + ROWS :, :] = jnp.zeros((PAD, full), F32)
    ext[PAD : PAD + ROWS, 0:LANES] = jnp.zeros((ROWS, LANES), F32)
    ext[PAD : PAD + ROWS, full - LANES :] = jnp.zeros((ROWS, LANES), F32)

    for load in loads:
        load.start()
    barrier = pltpu.get_barrier_semaphore()
    for d in range(1, visits):
        pl.semaphore_signal(barrier, inc=1, device_id={"visit": lax.rem(visit + d, visits)}, device_id_type=MESH)
    for d in range(1, members):
        pl.semaphore_signal(barrier, inc=1, device_id=member(d), device_id_type=MESH)
    pl.semaphore_wait(barrier, visits - 1 + members - 1)

    loads[0].wait()
    scatter = []
    for d in range(1, visits):
        to = lax.rem(visit + d, visits)
        copy = pltpu.make_async_remote_copy(
            src_ref=slot_ref.at[pl.ds(pl.multiple_of(to * chunk, chunk), chunk), :],
            dst_ref=landed.at[d - 1],
            send_sem=rs_send.at[d - 1],
            recv_sem=rs_recv.at[d - 1],
            device_id={"visit": to},
            device_id_type=MESH,
        )
        copy.start()
        scatter.append(copy)
    for load in loads[1:]:
        load.wait()
    groups = cells // 4
    lane = lax.broadcasted_iota(jnp.int32, (STAMP, LANES), 1)
    for q in range(groups):
        merged = jnp.zeros((STAMP, LANES), F32)
        for inner in range(4):
            g = 4 * q + inner
            first = LANES * (g // 2)
            block = image_ref[:, first : first + LANES]
            block = pltpu.roll(block, lax.rem(ROWS - offset_ref[0, 0, 0, g], ROWS), 0)[0:STAMP]
            move = lax.rem(2 * LANES + STAMP * inner - CELL * (g % 2) - offset_ref[1, 0, 0, g], LANES)
            merged = jnp.where(lane // STAMP == inner, pltpu.roll(block, move, 1), merged)
        stamps[NBASIS, :, LANES * q : LANES * (q + 1)] = merged
    for spare in range(NBASIS + 1, 32):
        stamps[spare] = jnp.zeros((STAMP, cells * STAMP), F32)

    owner = owner_ref[0, 0]
    current = jnp.where(owner == visit, slot_ref[own_rows, :], 0.0)
    for d in range(1, visits):
        scatter[d - 1].wait_recv()
        source = lax.rem(visit + visits - d, visits)
        current = jnp.where(owner == source, landed[d - 1], current)
    here = pl.ds(pl.multiple_of(PAD + visit * chunk, chunk), chunk)
    ext[here, LANES : LANES + width] = current
    gather = []
    for d in range(1, visits):
        copy = pltpu.make_async_remote_copy(
            src_ref=ext.at[here, pl.ds(LANES, width)],
            dst_ref=ext.at[here, pl.ds(LANES, width)],
            send_sem=ag_send.at[d - 1],
            recv_sem=ag_recv.at[d - 1],
            device_id={"visit": lax.rem(visit + d, visits)},
            device_id_type=MESH,
        )
        copy.start()
        gather.append(copy)
    for d in range(1, visits):
        source = lax.rem(visit + visits - d, visits)
        rows = pl.ds(pl.multiple_of(PAD + source * chunk, chunk), chunk)
        pltpu.make_async_remote_copy(
            src_ref=ext.at[rows, pl.ds(LANES, width)],
            dst_ref=ext.at[rows, pl.ds(LANES, width)],
            send_sem=ag_send.at[d - 1],
            recv_sem=ag_recv.at[d - 1],
            device_id={"visit": source},
            device_id_type=MESH,
        ).wait_recv()

    lane8 = lax.broadcasted_iota(jnp.int32, (8, LANES), 1) // PAD
    for side, (first, base) in enumerate(((LANES, 0), (width, LANES - PAD))):
        merged = jnp.zeros((8, LANES), F32)
        for r in range(ROWS // 8):
            block = ext[PAD + 8 * r : PAD + 8 * r + 8, first : first + LANES]
            merged = jnp.where(lane8 == r, pltpu.roll(block, (PAD * r - base) % LANES, 1), merged)
        edge[side] = merged
    row_span = {-1: (PAD, PAD + ROWS), 1: (ROWS, 0)}
    edges = []
    for way, (ds, dp) in enumerate(ways):
        if ds == 0:
            row_src, row_dst = row_span[dp]
            source = ext.at[pl.ds(row_src, PAD), pl.ds(LANES, width)]
            target = ext.at[pl.ds(row_dst, PAD), pl.ds(LANES, width)]
        else:
            source = edge.at[(ds + 1) // 2]
            target = edge_landed.at[way]
        copy = pltpu.make_async_remote_copy(
            src_ref=source,
            dst_ref=target,
            send_sem=ha_send.at[way],
            recv_sem=ha_recv.at[way],
            device_id=there(ds, dp),
            device_id_type=MESH,
        )
        edges.append(copy)

        @pl.when(exists(ds, dp))
        def _():
            copy.start()

    for copy in scatter:
        copy.wait_send()
    for copy in gather:
        copy.wait_send()
    for way, (ds, dp) in enumerate(ways):

        @pl.when(exists(-ds, -dp))
        def _():
            edges[way].wait_recv()
            if ds != 0:
                first, base = (full - LANES, 0) if ds < 0 else (0, LANES - PAD)
                spans = {0: (0, ROWS // 8, PAD), -1: (0, 2, PAD + ROWS), 1: (ROWS // 8 - 2, 2, 0)}
                group, number, row = spans[dp]
                packed = edge_landed[way]
                for r in range(number):
                    moved = pltpu.roll(packed, (base - PAD * (group + r)) % LANES, 1)
                    ext[row + 8 * r : row + 8 * r + 8, first : first + LANES] = moved

        @pl.when(exists(ds, dp))
        def _():
            edges[way].wait_send()

    shifted[0:ext_rows, :] = pltpu.roll(ext[...], full - (LANES - PAD), 1)
    shifted[ext_rows:, :] = jnp.zeros((8, full), F32)

    lane = lax.broadcasted_iota(jnp.int32, (CELL, LANES), 1)
    windows = []
    for h in range(cells // 2):
        parts = []
        for odd in range(2):
            g = 2 * h + odd
            block = shifted[:, LANES * h : LANES * h + 2 * LANES]
            block = pltpu.roll(block, ext_rows + 7 - offset_ref[0, 0, 0, g], 0)[0:CELL]
            move = 2 * LANES - offset_ref[1, 0, 0, g] - 1
            parts.append(pltpu.roll(block, move, 1)[:, 0:LANES])
        windows.append(jnp.where(lane < CELL, parts[0], parts[1]))
    window = jnp.concatenate(windows, axis=1)
    rows_done = dot3((srow[0], srow[1]), split2(window))
    stacked = jnp.concatenate([rows_done[:, 4 * CELL * q : 4 * CELL * (q + 1)] for q in range(groups)], axis=0)
    basis = dot3(split2(stacked), (scol[0], scol[1]))
    for q in range(groups):
        for b in range(ORDERS):
            first = (q * ORDERS + b) * STAMP
            for a in range(ORDERS):
                stamps[ORDERS * a + b, :, LANES * q : LANES * (q + 1)] = basis[first : first + STAMP, LANES * a : LANES * (a + 1)]
    spots = []
    at = 0
    for k in range(NBASIS):
        low = 8 * (k // 8)
        mine = stamps[k]
        for tile in range(low, 32, 8):
            pairs[at + tile - low : at + tile - low + 8, :] = jnp.sum(stamps[tile : tile + 8] * mine[None], axis=1)
        spots.append((at, 32 - low))
        at += 32 - low
    sums = pick_sum(pairs[...], lane_cell[...])
    rows = []
    for k, (at, length) in enumerate(spots):
        row = sums[at : at + length]
        place = lax.broadcasted_iota(jnp.int32, row.shape, 0) + (32 - length)
        row = jnp.where(place == NBASIS + 1, float(flux[k]), row)
        rows.append(row)
    padding = lax.broadcasted_iota(jnp.int32, (1, LANES), 1) >= cells
    diag = []
    for k, (at, length) in enumerate(spots):
        place = lax.broadcasted_iota(jnp.int32, rows[k].shape, 0) + (32 - length)
        diag.append(jnp.where(padding & (place == k), 1.0, rows[k]))
    weights, unit = eliminate(diag, flux)

    flux_col = jnp.concatenate([jnp.full((1, LANES), float(f), F32) for f in flux] + [jnp.zeros((7, LANES), F32)], axis=0)
    flux_cells = jnp.sum(weights * flux_col, axis=0, keepdims=True)
    curve_cells = jnp.sum(unit * flux_col, axis=0, keepdims=True)
    local = jnp.sum(jnp.where(padding, 0.0, flux_cells), axis=1, keepdims=True)
    sum_ref[...] = jnp.broadcast_to(local, (8, LANES))
    copies = []
    for d in range(1, members):
        copy = pltpu.make_async_remote_copy(
            src_ref=sum_ref,
            dst_ref=sum_landed.at[d - 1],
            send_sem=fx_send.at[d - 1],
            recv_sem=fx_recv.at[d - 1],
            device_id=member(d),
            device_id_type=MESH,
        )
        copy.start()
        copies.append(copy)

    both = jnp.concatenate([flux_cells, curve_cells, jnp.zeros((6, LANES), F32)], axis=0)
    spread = pick_sum(jnp.concatenate([weights, unit, both], axis=0), cell_lane[...])
    blocks = width // LANES
    windows = jnp.concatenate(
        [shifted[0:ext_rows, LANES * h : LANES * h + 2 * LANES] for h in range(blocks)], axis=0
    )
    columns = dot3(split2(windows), (fcol[0], fcol[1]))
    for which in range(2):
        for h in range(blocks):
            for b in range(ORDERS):
                acc = None
                for a in range(ORDERS):
                    k = 32 * which + ORDERS * a + b
                    term = spread[k : k + 1, LANES * h : LANES * (h + 1)] * columns[
                        ext_rows * h : ext_rows * (h + 1), LANES * a : LANES * (a + 1)
                    ]
                    acc = term if acc is None else acc + term
                high, low = split2(acc)
                spot = (slice(ext_rows * b, ext_rows * (b + 1)), slice(width * which + LANES * h, width * which + LANES * (h + 1)))
                combined_h[spot] = high
                combined_l[spot] = low
    matched = dot3((frow[0], frow[1]), (combined_h[...], combined_l[...]))
    total = sum_ref[...]
    for d in range(1, members):
        copies[d - 1].wait_recv()
        total = total + sum_landed[d - 1]
    mean_flux = total[0:1, 0:1] * (1.0 / (cells * members))
    correction = (mean_flux - spread[64:65]) / spread[65:66]
    out_ref[...] = image_ref[...] - matched[:, 0:width] - correction * matched[:, width:]
    for copy in copies:
        copy.wait_send()


def fused(owner, offsets, slot, image, filters, counts):
    width = image.shape[2]
    cells = width // CELL
    visits = counts[1]
    members = counts[0] * counts[2]
    sums = filters.sum(axis=1)
    flux = (sums[:, None] * sums[None, :]).reshape(-1)
    consts = constants(filters, cells)
    pair_rows = sum(32 - 8 * (k // 8) for k in range(NBASIS))
    deep = ORDERS * (ROWS + 2 * PAD)
    full = width + 2 * LANES
    dma = pltpu.SemaphoreType.DMA
    hbm = pl.BlockSpec(memory_space=pltpu.HBM)
    return pl.pallas_call(
        lambda *refs: fused_kernel(counts, flux, *refs),
        name="difference_patch",
        out_shape=jax.ShapeDtypeStruct((ROWS, width), F32),
        in_specs=[hbm] * (4 + len(consts)),
        out_specs=pl.BlockSpec(memory_space=pltpu.VMEM),
        scratch_shapes=[
            pltpu.SMEM(owner.shape, jnp.int32),
            pltpu.SMEM(offsets.shape, jnp.int32),
            pltpu.VMEM((ROWS, width), F32),
            pltpu.VMEM((ROWS, width), F32),
        ]
        + [pltpu.VMEM(const.shape, const.dtype) for const in consts]
        + [
            pltpu.VMEM((ROWS + 2 * PAD, full), F32),
            pltpu.VMEM((visits - 1, ROWS // visits, width), F32),
            pltpu.VMEM((2, 8, LANES), F32),
            pltpu.VMEM((8, 8, LANES), F32),
            pltpu.VMEM((ROWS + 2 * PAD + 8, full), F32),
            pltpu.VMEM((32, STAMP, cells * STAMP), F32),
            pltpu.VMEM((pair_rows, cells * STAMP), F32),
            pltpu.VMEM((deep, 2 * width), BF16),
            pltpu.VMEM((deep, 2 * width), BF16),
            pltpu.VMEM((8, LANES), F32),
            pltpu.VMEM((members - 1, 8, LANES), F32),
            dma((10,)),
            dma((visits - 1,)),
            dma((visits - 1,)),
            dma((visits - 1,)),
            dma((visits - 1,)),
            dma((8,)),
            dma((8,)),
            dma((members - 1,)),
            dma((members - 1,)),
        ],
        compiler_params=pltpu.CompilerParams(
            collective_id=0, has_side_effects=True, vmem_limit_bytes=40 << 20
        ),
    )(owner, *[pltpu.with_memory_space_constraint(v, pltpu.HBM) for v in (offsets, slot, image, *consts)])


def solution(mesh):
    counts = (mesh.shape["sky"], mesh.shape["visit"], mesh.shape["patch"])
    filters = filter_bank()

    def body(template_store, science, owner_visit, stamp_offset):
        return fused(owner_visit, stamp_offset, template_store, science, filters, counts)[None]

    spec = P("visit", "patch", "sky")
    in_specs = (spec, spec, P("sky", "patch"), P(None, "visit", "patch", "sky"))
    return jax.shard_map(body, mesh=mesh, in_specs=in_specs, out_specs=spec, check_vma=False)
```
